32 devices in a mesh: dp: 16 (over z, x, core), mp: 2 (over y).
Axes of the slice: x: 2, y: 2, z: 4, core: 2. Of those that a mesh axis runs over, the one named last changes fastest.
Arguments:
- activations: float32 [32, 736, 1152], P('dp', 'mp'), may hold values from -6 to 6
- valid_mask: int32 [32, 736], P('dp'), may hold values from 0 to 1, as said below
- first_gain: float32 [1152], replicated, may hold values from 0.25 to 1.75
- first_shift: float32 [1152], replicated, may hold values from -3 to 3
- w_query: float32 [1152, 1152], P('dp', 'mp'), may hold values from -0.1875 to 0.1875
- b_query: float32 [1152], replicated, may hold values from -3 to 3
- w_key: float32 [1152, 1152], P('dp', 'mp'), may hold values from -0.1875 to 0.1875
- w_value: float32 [1152, 1152], P('dp', 'mp'), may hold values from -0.1875 to 0.1875
- b_value: float32 [1152], replicated, may hold values from -1.5 to 1.5
- w_out: float32 [1152, 1152], P('mp', 'dp'), may hold values from -0.1875 to 0.1875
- b_out: float32 [1152], replicated, may hold values from -1.5 to 1.5
- second_gain: float32 [1152], replicated, may hold values from 0.25 to 1.75
- second_shift: float32 [1152], replicated, may hold values from -3 to 3
- w_up: float32 [1152, 4304], P('dp', 'mp'), may hold values from -0.1875 to 0.1875
- b_up: float32 [4304], replicated, may hold values from -3 to 3
- w_down: float32 [4304, 1152], P('mp', 'dp'), may hold values from -0.1875 to 0.1875
- b_down: float32 [1152], replicated, may hold values from -3 to 3
- cotangent: float32 [32, 736, 1152], P('dp', 'mp'), may hold values from -6 to 6
Outputs:
- output: float32 [32, 736, 1152], P('dp', 'mp')
- grad_activations: float32 [32, 736, 1152], P('dp', 'mp')
- grad_first_gain: float32 [1152], replicated
- grad_first_shift: float32 [1152], replicated
- grad_w_query: float32 [1152, 1152], P('dp', 'mp')
- grad_b_query: float32 [1152], replicated
- grad_w_key: float32 [1152, 1152], P('dp', 'mp')
- grad_w_value: float32 [1152, 1152], P('dp', 'mp')
- grad_b_value: float32 [1152], replicated
- grad_w_out: float32 [1152, 1152], P('mp', 'dp')
- grad_b_out: float32 [1152], replicated
- grad_second_gain: float32 [1152], replicated
- grad_second_shift: float32 [1152], replicated
- grad_w_up: float32 [1152, 4304], P('dp', 'mp')
- grad_b_up: float32 [4304], replicated
- grad_w_down: float32 [4304, 1152], P('mp', 'dp')
- grad_b_down: float32 [1152], replicated
The draws below stay inside these ranges and needn't reach their ends.
Inputs may be any that keep to these rules, and one draw needn't show every extreme that they name: `valid_mask`: each image is either empty (all zeros) or has ones at exactly its first 729 positions and zeros after; 8 images, drawn at random, are empty.
All inputs are finite; a program needn't handle non-finite values.
Results may differ from the reference program's by a relative error of at most 0.02.
Values may be sent and summed in bfloat16 or wider, within the bound.
No kernel may reach another device: no remote copies, remote signals or barrier semaphores. Data moves between devices by JAX's collectives and lax.ppermute only.
A program may use at most 192 MiB of HBM per device.

```python
import jax
import jax.numpy as jnp
from jax import lax

D = 1152
HEADS = 16
HEAD_DIM = 72
FF = 4304
PATCH = 729
SEQ = 736
IMAGES = 32
N_MP = 2


def draw_valid_mask(key, part):
    order = jax.random.permutation(key, IMAGES)
    filled = (order >= IMAGES // 4).astype(jnp.int32)
    place = lax.broadcasted_iota(jnp.int32, (IMAGES, SEQ), 1)
    return filled[:, None] * (place < PATCH).astype(jnp.int32)


def block_scale(rng, extent, pieces, low, top_value):
    def one(dim, parts):
        draws = jax.random.uniform(jax.random.fold_in(jax.random.fold_in(rng, 6), dim), (parts,), jnp.float32, low / len(pieces), top_value / len(pieces))
        return jnp.repeat(jnp.exp(draws), extent[dim] // parts).reshape((-1,) + (1,) * (len(extent) - dim - 1))

    gain = one(*pieces[0])
    for cut in pieces[1:]:
        gain = gain * one(*cut)
    return gain


def noise(rng, extent, deviation, limit, pieces=(), dtype=jnp.bfloat16):
    array = jax.random.normal(rng, extent, jnp.float32) * deviation
    if len(pieces) > 0:
        array = block_scale(rng, extent, pieces, -0.22, 0.18) * array
    return jnp.clip(array, min=-limit, max=limit).astype(dtype)


def setup_inputs(seed: int = 0) -> dict:
    seeds = jax.random.split(jax.random.key(seed), 19)
    return {
        "activations": noise(seeds[0], (IMAGES, SEQ, D), 1.0, 6.0, ((0, 16), (1, 2)), jnp.float32),
        "valid_mask": draw_valid_mask(jax.random.fold_in(seeds[18], 71), 0),
        "first_gain": jnp.clip(1.0 + 0.15 * jax.random.normal(seeds[2], (D,), jnp.float32), 0.25, 1.75),
        "first_shift": noise(seeds[3], (D,), 0.5, 3.0, (), jnp.float32),
        "w_query": noise(seeds[4], (D, D), D ** -0.5, 0.1875, ((0, 16), (1, 2)), jnp.float32),
        "b_query": noise(seeds[5], (D,), 0.5, 3.0, (), jnp.float32),
        "w_key": noise(seeds[6], (D, D), D ** -0.5, 0.1875, ((0, 16), (1, 2)), jnp.float32),
        "w_value": noise(seeds[7], (D, D), D ** -0.5, 0.1875, ((0, 16), (1, 2)), jnp.float32),
        "b_value": noise(seeds[8], (D,), 0.25, 1.5, (), jnp.float32),
        "w_out": noise(seeds[9], (D, D), D ** -0.5, 0.1875, ((0, 2), (1, 16)), jnp.float32),
        "b_out": noise(seeds[10], (D,), 0.25, 1.5, (), jnp.float32),
        "second_gain": jnp.clip(1.0 + 0.15 * jax.random.normal(seeds[11], (D,), jnp.float32), 0.25, 1.75),
        "second_shift": noise(seeds[12], (D,), 0.5, 3.0, (), jnp.float32),
        "w_up": noise(seeds[13], (D, FF), D ** -0.5, 0.1875, ((0, 16), (1, 2)), jnp.float32),
        "b_up": noise(seeds[14], (FF,), 0.5, 3.0, (), jnp.float32),
        "w_down": noise(seeds[15], (FF, D), (FF // 4) ** -0.5, 0.1875, ((0, 2), (1, 16)), jnp.float32),
        "b_down": noise(seeds[16], (D,), 0.5, 3.0, (), jnp.float32),
        "cotangent": noise(seeds[17], (IMAGES, SEQ, D), 1.0, 6.0, ((0, 16), (1, 2)), jnp.float32),
    }


EPS = 1e-06
HIGH = lax.Precision.HIGHEST

@jax.custom_vjp
def low(v):
    return lax.optimization_barrier(v.astype(jnp.bfloat16)).astype(jnp.float32)

@jax.custom_vjp
def low_back(v):
    return v

def low_keep(v):
    return (low(v), None)

def low_pass(kept, grad):
    return (grad,)

def back_keep(v):
    return (v, None)

def back_low(kept, grad):
    return (low(grad),)
low.defvjp(low_keep, low_pass)
low_back.defvjp(back_keep, back_low)

def layer_norm(tensor, norm_gain, norm_shift):
    average = lax.optimization_barrier(jnp.mean(tensor, -1, keepdims=True))
    centred = tensor - average
    spread = lax.optimization_barrier(jnp.mean(centred * centred, -1, keepdims=True))
    return centred * lax.rsqrt(spread + EPS) * norm_gain + norm_shift

def matmul(left_side, right_side):
    return jnp.dot(left_side, right_side, precision=HIGH, preferred_element_type=jnp.float32)

def attend_image(image_block):
    queries, key_rows, values, validity = image_block
    head_q = queries.reshape(SEQ, HEADS, HEAD_DIM)
    head_k = key_rows.reshape(SEQ, HEADS, HEAD_DIM)
    head_v = values.reshape(SEQ, HEADS, HEAD_DIM)
    raw_scores = low_back(jnp.einsum('qhd,khd->hqk', head_q, head_k, precision=HIGH))
    unnorm = validity[None, None, :] * jnp.exp(raw_scores * HEAD_DIM ** (-0.5))
    row_total = jnp.maximum(lax.optimization_barrier(jnp.sum(unnorm, -1, keepdims=True)), 1.0)
    attention = low(unnorm / row_total)
    mixture = jnp.einsum('hqk,khd->qhd', attention, head_v, precision=HIGH)
    return mixture.reshape(SEQ, D)

def reference(activations, valid_mask, first_gain, first_shift, w_query, b_query, w_key, w_value, b_value, w_out, b_out, second_gain, second_shift, w_up, b_up, w_down, b_down, cotangent):
    validity = valid_mask.astype(jnp.float32)
    images = activations.shape[0]
    shape = (images, SEQ, D)
    head_width = D // N_MP
    unit_width = FF // N_MP

    def forward(tokens, gain_one, shift_one, query_w, query_b, key_w, value_w, value_b, out_w, out_b, gain_two, shift_two, up_w, up_b, down_w, down_b):
        flat = tokens.reshape(-1, D)
        input_one = low(layer_norm(flat, gain_one, shift_one))
        query_low = low(query_w)
        key_low = low(key_w)
        value_low = low(value_w)
        out_low = low(out_w)
        up_low = low(up_w)
        down_low = low(down_w)
        query_parts = []
        key_parts = []
        value_parts = []
        for group in range(N_MP):
            copy_one = low_back(input_one)
            begin = group * head_width
            query_parts.append(matmul(copy_one, query_low[:, begin:begin + head_width]))
            key_parts.append(matmul(copy_one, key_low[:, begin:begin + head_width]))
            value_parts.append(matmul(copy_one, value_low[:, begin:begin + head_width]))
        queries = low_back(low(jnp.concatenate(query_parts, -1) + query_b))
        key_rows = low_back(low(jnp.concatenate(key_parts, -1)))
        values = low_back(low(jnp.concatenate(value_parts, -1) + value_b))
        mixed = lax.map(jax.checkpoint(attend_image), (queries.reshape(shape), key_rows.reshape(shape), values.reshape(shape), validity))
        mixture = low_back(low(mixed.reshape(-1, D)))
        attn_total = jnp.zeros_like(flat)
        for group in range(N_MP):
            begin = group * head_width
            attn_total = attn_total + low(matmul(mixture[:, begin:begin + head_width], out_low[begin:begin + head_width, :]))
        residual = flat + low_back(attn_total) + out_b
        input_two = low(layer_norm(residual, gain_two, shift_two))
        hidden_parts = []
        for group in range(N_MP):
            copy_two = low_back(input_two)
            begin = group * unit_width
            hidden_parts.append(matmul(copy_two, up_low[:, begin:begin + unit_width]))
        hidden = low_back(jnp.concatenate(hidden_parts, -1) + up_b)
        active = low(jax.nn.gelu(hidden, approximate=True))
        mlp_total = jnp.zeros_like(flat)
        for group in range(N_MP):
            begin = group * unit_width
            mlp_total = mlp_total + low(matmul(active[:, begin:begin + unit_width], down_low[begin:begin + unit_width, :]))
        result = residual + low_back(mlp_total) + down_b
        return result.reshape(shape)
    output, pullback = jax.vjp(forward, activations, first_gain, first_shift, w_query, b_query, w_key, w_value, b_value, w_out, b_out, second_gain, second_shift, w_up, b_up, w_down, b_down)
    grads = pullback(cotangent * validity[:, :, None])
    return (output, grads[0], grads[1], grads[2], grads[3], grads[4], grads[5], grads[6], grads[7], grads[8], grads[9], grads[10], grads[11], grads[12], grads[13], grads[14], grads[15])
```

```python
import jax
import jax.numpy as jnp
from jax import lax
from jax.experimental import pallas as pl
from jax.experimental.layout import Layout, with_layout_constraint
from jax.sharding import PartitionSpec as P

HEAD_DIM = 72


EPS = 1e-06


def normalize(tensor):
    average = jnp.mean(tensor, -1, keepdims=True)
    centred = tensor - average
    spread = jnp.mean(centred * centred, -1, keepdims=True)
    inverse = lax.rsqrt(spread + EPS)
    return (centred * inverse, inverse)


def norm_back(grad_norm, normed, inverse, norm_gain):
    scaled = grad_norm * norm_gain
    first_mean = jnp.mean(scaled, -1, keepdims=True)
    second_mean = jnp.mean(scaled * normed, -1, keepdims=True)
    return inverse * (scaled - first_mean - normed * second_mean)


def flat_rows(tensor):
    return tensor.reshape(-1, tensor.shape[-1])


def right_dot(left_side, right_side):
    return jnp.dot(flat_rows(left_side), right_side, preferred_element_type=jnp.float32)


def inner_dot(left_side, right_side):
    return lax.dot_general(
        flat_rows(left_side),
        flat_rows(right_side),
        (((0,), (0,)), ((), ())),
        preferred_element_type=jnp.float32,
    )


def transposed_dot(left_side, right_side):
    return lax.dot_general(
        flat_rows(left_side),
        right_side,
        (((1,), (1,)), ((), ())),
        preferred_element_type=jnp.float32,
    )


def activate(hidden):
    return jax.nn.gelu(hidden, approximate=True)


def collect(tensor):
    return lax.all_gather(tensor, "mp", axis=1, tiled=True)


def collect_again(tensor):
    return lax.all_gather(tensor, "mp", axis=1, tiled=True)


def spread_sum(tensor):
    return lax.psum_scatter(
        tensor.astype(jnp.bfloat16), "mp", scatter_dimension=1, tiled=True
    ).astype(jnp.float32)


def widen(vector, length, mp_index):
    return lax.dynamic_update_slice_in_dim(
        jnp.zeros((length,), jnp.float32), vector, mp_index * vector.shape[0], 0
    )


def project(rows, query_full, key_full, value_full, query_bias, value_bias):
    shape = rows.shape[:2] + (query_full.shape[1],)
    queries = (right_dot(rows, query_full) + query_bias).astype(jnp.bfloat16).reshape(shape)
    key_rows = right_dot(rows, key_full).astype(jnp.bfloat16).reshape(shape)
    values = (right_dot(rows, value_full) + value_bias).astype(jnp.bfloat16).reshape(shape)
    return (queries, key_rows, values)


def expand(rows, up_full, up_bias):
    hidden = right_dot(rows, up_full) + up_bias
    return (hidden, activate(hidden).astype(jnp.bfloat16))


def split_heads(tensor):
    return tensor.reshape(tensor.shape[0], tensor.shape[1] // HEAD_DIM, HEAD_DIM)


def scores_of(queries, key_rows):
    raw_scores = jnp.einsum(
        "qhd,khd->hqk",
        split_heads(queries),
        split_heads(key_rows),
        preferred_element_type=jnp.float32,
    )
    return raw_scores * HEAD_DIM ** (-0.5)


def attend_forward(image_block):
    queries, key_rows, values, validity = image_block
    unnorm = validity[None, None, :] * jnp.exp(scores_of(queries, key_rows))
    row_total = jnp.maximum(jnp.sum(unnorm, -1, keepdims=True), 1.0)
    attention = (unnorm / row_total).astype(jnp.bfloat16)
    mixture = jnp.einsum(
        "hqk,khd->qhd", attention, split_heads(values), preferred_element_type=jnp.float32
    )
    return (mixture.reshape(queries.shape).astype(jnp.bfloat16), jnp.log(row_total))


def attend_back(image_block):
    queries, key_rows, values, validity, log_total, grad_mixture = image_block
    attention = validity[None, None, :] * jnp.exp(scores_of(queries, key_rows) - log_total)
    bound = (log_total > 0.0).astype(jnp.float32)
    grad_heads = split_heads(grad_mixture)
    grad_attention = jnp.einsum(
        "qhd,khd->hqk", grad_heads, split_heads(values), preferred_element_type=jnp.float32
    )
    row_delta = bound * jnp.sum(attention * grad_attention, -1, keepdims=True)
    grad_scores = (attention * (grad_attention - row_delta) * HEAD_DIM ** (-0.5)).astype(
        jnp.bfloat16
    )
    grad_queries = jnp.einsum(
        "hqk,khd->qhd", grad_scores, split_heads(key_rows), preferred_element_type=jnp.float32
    )
    grad_keys = jnp.einsum(
        "hqk,qhd->khd", grad_scores, split_heads(queries), preferred_element_type=jnp.float32
    )
    grad_values = jnp.einsum(
        "hqk,qhd->khd",
        attention.astype(jnp.bfloat16),
        grad_heads,
        preferred_element_type=jnp.float32,
    )
    shape = queries.shape
    return (
        grad_queries.reshape(shape).astype(jnp.bfloat16),
        grad_keys.reshape(shape).astype(jnp.bfloat16),
        grad_values.reshape(shape).astype(jnp.bfloat16),
    )


def local(
    activations,
    valid_mask,
    first_gain,
    first_shift,
    w_query,
    b_query,
    w_key,
    w_value,
    b_value,
    w_out,
    b_out,
    second_gain,
    second_shift,
    w_up,
    b_up,
    w_down,
    b_down,
    cotangent,
):
    images, local_rows, width = activations.shape
    mp_index = lax.axis_index("mp")
    head_cols = w_query.shape[1]
    hidden_cols = w_up.shape[1]
    validity = valid_mask.astype(jnp.float32)
    row_valid = lax.dynamic_slice_in_dim(validity, mp_index * local_rows, local_rows, 1)
    query_bias = lax.dynamic_slice_in_dim(b_query, mp_index * head_cols, head_cols)
    value_bias = lax.dynamic_slice_in_dim(b_value, mp_index * head_cols, head_cols)
    up_bias = lax.dynamic_slice_in_dim(b_up, mp_index * hidden_cols, hidden_cols)
    low_type = jnp.bfloat16
    normed_one, inverse_one = normalize(activations)
    input_one = (normed_one * first_gain + first_shift).astype(low_type)
    query_full, key_full, value_full, out_full = (
        lax.all_gather(w_query.astype(low_type), "dp", axis=0, tiled=True),
        lax.all_gather(w_key.astype(low_type), "dp", axis=0, tiled=True),
        lax.all_gather(w_value.astype(low_type), "dp", axis=0, tiled=True),
        lax.all_gather(w_out.astype(low_type), "dp", axis=1, tiled=True),
    )
    rows_one = collect(input_one)
    queries, key_rows, values = project(
        rows_one, query_full, key_full, value_full, query_bias, value_bias
    )
    mixture, log_total = lax.map(attend_forward, (queries, key_rows, values, validity))
    attn_part = right_dot(mixture, out_full).reshape(rows_one.shape)
    residual = activations + spread_sum(attn_part) + b_out
    normed_two, inverse_two = normalize(residual)
    input_two = (normed_two * second_gain + second_shift).astype(low_type)
    up_full, down_full = (
        lax.all_gather(w_up.astype(low_type), "dp", axis=0, tiled=True),
        lax.all_gather(w_down.astype(low_type), "dp", axis=1, tiled=True),
    )
    rows_two = collect(input_two)
    hidden, active = expand(rows_two, up_full, up_bias)
    mlp_part = jnp.dot(active, down_full, preferred_element_type=jnp.float32).reshape(
        rows_two.shape
    )
    output = residual + spread_sum(mlp_part) + b_down
    grad_out = cotangent * row_valid[:, :, None]
    grad_b_down = jnp.sum(grad_out, (0, 1))
    grad_rows_two = collect(grad_out.astype(low_type))
    up_back, down_back = (
        lax.all_gather(w_up.astype(low_type), "dp", axis=0, tiled=True),
        lax.all_gather(w_down.astype(low_type), "dp", axis=1, tiled=True),
    )
    rows_two_back = collect_again(input_two)
    hidden_back, active_back = expand(rows_two_back, up_back, up_bias)
    grad_w_down = inner_dot(active_back, grad_rows_two)
    grad_active = transposed_dot(grad_rows_two, down_back)
    grad_hidden = jax.vjp(activate, hidden_back)[1](grad_active)[0].astype(low_type)
    grad_b_up_here = jnp.sum(grad_hidden.astype(jnp.float32), 0)
    grad_w_up = inner_dot(rows_two_back, grad_hidden)
    grad_input_two = spread_sum(transposed_dot(grad_hidden, up_back).reshape(rows_two.shape))
    grad_second_gain = jnp.sum(grad_input_two * normed_two, (0, 1))
    grad_second_shift = jnp.sum(grad_input_two, (0, 1))
    grad_residual = grad_out + norm_back(grad_input_two, normed_two, inverse_two, second_gain)
    grad_b_out = jnp.sum(grad_residual, (0, 1))
    grad_rows_one = collect(grad_residual.astype(low_type))
    query_back, key_back, value_back, out_back = (
        lax.all_gather(w_query.astype(low_type), "dp", axis=0, tiled=True),
        lax.all_gather(w_key.astype(low_type), "dp", axis=0, tiled=True),
        lax.all_gather(w_value.astype(low_type), "dp", axis=0, tiled=True),
        lax.all_gather(w_out.astype(low_type), "dp", axis=1, tiled=True),
    )
    rows_one_back = collect_again(input_one)
    queries_back, key_rows_back, values_back = project(
        rows_one_back, query_back, key_back, value_back, query_bias, value_bias
    )
    mixture_back, log_total_back = lax.map(
        attend_forward, (queries_back, key_rows_back, values_back, validity)
    )
    grad_w_out = inner_dot(mixture_back, grad_rows_one)
    grad_mixture = (
        transposed_dot(grad_rows_one, out_back).astype(low_type).reshape(queries_back.shape)
    )
    grad_queries, grad_keys, grad_values = lax.map(
        attend_back,
        (queries_back, key_rows_back, values_back, validity, log_total_back, grad_mixture),
    )
    grad_w_query = inner_dot(rows_one_back, grad_queries)
    grad_w_key = inner_dot(rows_one_back, grad_keys)
    grad_w_value = inner_dot(rows_one_back, grad_values)
    grad_b_query_here = jnp.sum(grad_queries.astype(jnp.float32), (0, 1))
    grad_b_value_here = jnp.sum(grad_values.astype(jnp.float32), (0, 1))
    grad_input_part = (
        transposed_dot(grad_queries, query_back)
        + transposed_dot(grad_keys, key_back)
        + transposed_dot(grad_values, value_back)
    )
    grad_input_one = spread_sum(grad_input_part.reshape(rows_one.shape))
    grad_first_gain = jnp.sum(grad_input_one * normed_one, (0, 1))
    grad_first_shift = jnp.sum(grad_input_one, (0, 1))
    grad_activations = grad_residual + norm_back(
        grad_input_one, normed_one, inverse_one, first_gain
    )
    (
        grad_w_query_shard,
        grad_w_key_shard,
        grad_w_value_shard,
        grad_w_out_shard,
        grad_w_up_shard,
        grad_w_down_shard,
    ) = (
        lax.psum_scatter(
            grad_w_query.astype(jnp.bfloat16), "dp", scatter_dimension=0, tiled=True
        ).astype(jnp.float32),
        lax.psum_scatter(
            grad_w_key.astype(jnp.bfloat16), "dp", scatter_dimension=0, tiled=True
        ).astype(jnp.float32),
        lax.psum_scatter(
            grad_w_value.astype(jnp.bfloat16), "dp", scatter_dimension=0, tiled=True
        ).astype(jnp.float32),
        lax.psum_scatter(
            grad_w_out.astype(jnp.bfloat16), "dp", scatter_dimension=1, tiled=True
        ).astype(jnp.float32),
        lax.psum_scatter(
            grad_w_up.astype(jnp.bfloat16), "dp", scatter_dimension=0, tiled=True
        ).astype(jnp.float32),
        lax.psum_scatter(
            grad_w_down.astype(jnp.bfloat16), "dp", scatter_dimension=1, tiled=True
        ).astype(jnp.float32),
    )
    vector_sums = lax.psum(
        (
            grad_first_gain,
            grad_first_shift,
            widen(grad_b_query_here, b_query.shape[0], mp_index),
            widen(grad_b_value_here, b_value.shape[0], mp_index),
            grad_b_out,
            grad_second_gain,
            grad_second_shift,
            widen(grad_b_up_here, b_up.shape[0], mp_index),
            grad_b_down,
        ),
        ("dp", "mp"),
    )
    return (
        output,
        grad_activations,
        vector_sums[0],
        vector_sums[1],
        grad_w_query_shard,
        vector_sums[2],
        grad_w_key_shard,
        grad_w_value_shard,
        vector_sums[3],
        grad_w_out_shard,
        vector_sums[4],
        vector_sums[5],
        vector_sums[6],
        grad_w_up_shard,
        vector_sums[7],
        grad_w_down_shard,
        vector_sums[8],
    )


SCALE = HEAD_DIM ** (-0.5)
LOW = jnp.bfloat16


def swap(tensor):
    return lax.ppermute(tensor, "mp", [(0, 1), (1, 0)])


def dot_rows(left_side, right_side):
    return lax.dot_general(
        left_side, right_side, (((1,), (0,)), ((), ())), preferred_element_type=jnp.float32
    )


def dot_last(left_side, right_side):
    return lax.dot_general(
        left_side, right_side, (((1,), (1,)), ((), ())), preferred_element_type=jnp.float32
    )


def dot_first(left_side, right_side):
    return lax.dot_general(
        left_side, right_side, (((0,), (0,)), ((), ())), preferred_element_type=jnp.float32
    )


def attention_kernel(valid_ref, own_ref, other_ref, mix_own_ref, mix_other_ref):
    width = mix_own_ref.shape[1]
    valid = valid_ref[0]
    for head in range(width // HEAD_DIM):
        cols = slice(head * HEAD_DIM, (head + 1) * HEAD_DIM)
        key_cols = slice(width + head * HEAD_DIM, width + (head + 1) * HEAD_DIM)
        value_cols = slice(2 * width + head * HEAD_DIM, 2 * width + (head + 1) * HEAD_DIM)
        keys = jnp.concatenate([own_ref[:, key_cols], other_ref[:, key_cols]], 0)
        values = jnp.concatenate([own_ref[:, value_cols], other_ref[:, value_cols]], 0)
        for source, target in ((own_ref, mix_own_ref), (other_ref, mix_other_ref)):
            unnorm = jnp.exp(dot_last(source[:, cols], keys) * SCALE) * valid
            row_total = jnp.maximum(jnp.sum(unnorm, -1, keepdims=True), 1.0)
            attention = (unnorm * (1.0 / row_total)).astype(LOW)
            target[:, cols] = dot_rows(attention, values).astype(LOW)


def attention_forward(valid_rows, own, other, image, width):
    rows = own.shape[0] // valid_rows.shape[0]
    block = pl.BlockSpec((rows, own.shape[1]), lambda step: (image, 0))
    mix_block = pl.BlockSpec((rows, width), lambda step: (0, 0))
    mix_shape = jax.ShapeDtypeStruct((rows, width), LOW)
    return pl.pallas_call(
        attention_kernel,
        grid=(1,),
        in_specs=[pl.BlockSpec((1, 1, 2 * rows), lambda step: (image, 0, 0)), block, block],
        out_specs=[mix_block, mix_block],
        out_shape=[mix_shape, mix_shape],
        name="attention_forward",
    )(valid_rows, own, other)


def attention_back_kernel(
    valid_ref, own_ref, other_ref, grad_own_ref, grad_other_ref, out_own_ref, out_other_ref
):
    rows, width = grad_own_ref.shape
    valid = valid_ref[0]
    for head in range(width // HEAD_DIM):
        cols = slice(head * HEAD_DIM, (head + 1) * HEAD_DIM)
        key_cols = slice(width + head * HEAD_DIM, width + (head + 1) * HEAD_DIM)
        value_cols = slice(2 * width + head * HEAD_DIM, 2 * width + (head + 1) * HEAD_DIM)
        keys = jnp.concatenate([own_ref[:, key_cols], other_ref[:, key_cols]], 0)
        values = jnp.concatenate([own_ref[:, value_cols], other_ref[:, value_cols]], 0)
        keys_turned = keys.T
        grad_keys = None
        grad_values = None
        for source, grad_source, target in (
            (own_ref, grad_own_ref, out_own_ref),
            (other_ref, grad_other_ref, out_other_ref),
        ):
            queries = source[:, cols]
            grad_mix = grad_source[:, cols]
            unnorm = jnp.exp(dot_last(keys, queries) * SCALE) * valid
            row_total = jnp.maximum(jnp.sum(unnorm, 0, keepdims=True), 1.0)
            attention = unnorm * (1.0 / row_total)
            bound = jnp.where(row_total > 1.0, 1.0, 0.0)
            grad_attention = dot_last(values, grad_mix)
            row_delta = bound * jnp.sum(attention * grad_attention, 0, keepdims=True)
            grad_scores = (attention * (grad_attention - row_delta) * SCALE).astype(LOW)
            grad_turned = dot_rows(keys_turned, grad_scores)
            target[:, cols] = grad_turned.T.astype(LOW)
            add_keys = dot_rows(grad_scores, queries)
            add_values = dot_rows(attention.astype(LOW), grad_mix)
            grad_keys = add_keys if grad_keys is None else grad_keys + add_keys
            grad_values = add_values if grad_values is None else grad_values + add_values
        grad_keys = grad_keys.astype(LOW)
        grad_values = grad_values.astype(LOW)
        out_own_ref[:, key_cols] = grad_keys[:rows]
        out_other_ref[:, key_cols] = grad_keys[rows:]
        out_own_ref[:, value_cols] = grad_values[:rows]
        out_other_ref[:, value_cols] = grad_values[rows:]


def attention_back(valid_cols, own, other, grad_own, grad_other):
    images = valid_cols.shape[0]
    rows = own.shape[0] // images
    block = pl.BlockSpec((rows, own.shape[1]), lambda step: (step, 0))
    grad_block = pl.BlockSpec((rows, grad_own.shape[1]), lambda step: (step, 0))
    out_shape = jax.ShapeDtypeStruct(own.shape, LOW)
    return pl.pallas_call(
        attention_back_kernel,
        grid=(images,),
        in_specs=[
            pl.BlockSpec((1, 2 * rows, 1), lambda step: (step, 0, 0)),
            block,
            block,
            grad_block,
            grad_block,
        ],
        out_specs=[block, block],
        out_shape=[out_shape, out_shape],
        name="attention_back",
    )(valid_cols, own, other, grad_own, grad_other)


def pad_cols(tensor, width):
    return jnp.pad(tensor, ((0, 0), (0, width - tensor.shape[1])))


def gather_rows(tensor):
    return lax.all_gather(tensor, "dp", axis=0, tiled=True)


def scatter_rows(tensor):
    tensor = with_layout_constraint(tensor, Layout((0, 1)))
    part = lax.psum_scatter(tensor, "dp", scatter_dimension=0, tiled=True)
    return with_layout_constraint(part, Layout((0, 1))).astype(jnp.float32)


def local_pair(
    activations,
    valid_mask,
    first_gain,
    first_shift,
    w_query,
    b_query,
    w_key,
    w_value,
    b_value,
    w_out,
    b_out,
    second_gain,
    second_shift,
    w_up,
    b_up,
    w_down,
    b_down,
    cotangent,
):
    images, half, width = activations.shape
    mp_index = lax.axis_index("mp")
    cols = w_query.shape[1]
    units = w_up.shape[1]
    lane_units = -(-units // 128) * 128
    lane_qkv = -(-3 * cols // 128) * 128
    tokens = images * half
    validity = valid_mask.astype(jnp.float32)
    valid_own = lax.dynamic_slice_in_dim(validity, mp_index * half, half, 1)
    valid_other = lax.dynamic_slice_in_dim(validity, (1 - mp_index) * half, half, 1)
    valid_both = jnp.concatenate([valid_own, valid_other], 1)
    query_bias = lax.dynamic_slice_in_dim(b_query, mp_index * cols, cols)
    value_bias = lax.dynamic_slice_in_dim(b_value, mp_index * cols, cols)
    up_bias = lax.dynamic_slice_in_dim(b_up, mp_index * units, units)
    qkv_bias = jnp.concatenate([query_bias, jnp.zeros_like(query_bias), value_bias])

    qkv_shard = jnp.concatenate([w_query, w_key, w_value], 1).astype(LOW)
    first_full = gather_rows(
        jnp.concatenate([pad_cols(qkv_shard, lane_qkv), w_out.T.astype(LOW)], 1)
    )
    qkv_full = first_full[:, : 3 * cols]
    out_full = first_full[:, lane_qkv:]
    second_full = gather_rows(
        jnp.concatenate(
            [pad_cols(w_up.astype(LOW), lane_units), w_down.T.astype(LOW)], 1
        )
    )
    up_full = second_full[:, :units]
    down_full = second_full[:, lane_units:]

    flat = activations.reshape(tokens, width)
    normed_one, inverse_one = normalize(flat)
    input_own = (normed_one * first_gain + first_shift).astype(LOW)
    input_other = swap(input_own)
    grad_out = (cotangent * valid_own[:, :, None]).reshape(tokens, width)
    grad_b_down = jnp.sum(grad_out, 0)
    grad_out_low = grad_out.astype(LOW)
    grad_rows = jnp.concatenate([grad_out_low, swap(grad_out_low)], 0)

    qkv_own = (dot_rows(input_own, qkv_full) + qkv_bias).astype(LOW)
    qkv_other = (dot_rows(input_other, qkv_full) + qkv_bias).astype(LOW)

    mix_own, mix_other, residuals, normeds, inverses, lows, crossed = [], [], [], [], [], [], []
    for image in range(images):
        own, other = attention_forward(valid_both[:, None, :], qkv_own, qkv_other, image, cols)
        mix_own.append(own)
        mix_other.append(other)
        received = swap(dot_last(other, out_full).astype(LOW)).astype(jnp.float32)
        residual = activations[image] + (dot_last(own, out_full) + received) + b_out
        normed, inverse = normalize(residual)
        low_rows = (normed * second_gain + second_shift).astype(LOW)
        residuals.append(residual)
        normeds.append(normed)
        inverses.append(inverse)
        lows.append(low_rows)
        crossed.append(swap(low_rows))
    residual = jnp.concatenate(residuals, 0)
    normed_two = jnp.concatenate(normeds, 0)
    inverse_two = jnp.concatenate(inverses, 0)
    rows_two = jnp.concatenate(lows + crossed, 0)

    hidden = dot_rows(rows_two, up_full) + up_bias
    active = activate(hidden).astype(LOW)
    grad_active = dot_rows(grad_rows, down_full)
    grad_hidden = jax.vjp(activate, hidden)[1](grad_active)[0].astype(LOW)
    back_other = swap(dot_last(grad_hidden[tokens:], up_full).astype(LOW))
    back_own = dot_last(grad_hidden[:tokens], up_full)
    grad_b_up_here = jnp.sum(grad_hidden.astype(jnp.float32), 0)
    grad_down_part = dot_first(grad_rows, active).astype(LOW)
    grad_up_part = dot_first(rows_two, grad_hidden).astype(LOW)

    mlp_other = swap(dot_last(active[tokens:], down_full).astype(LOW)).astype(jnp.float32)
    output = residual + (dot_last(active[:tokens], down_full) + mlp_other) + b_down

    grad_input_two = back_own + back_other.astype(jnp.float32)
    grad_second_gain = jnp.sum(grad_input_two * normed_two, 0)
    grad_second_shift = jnp.sum(grad_input_two, 0)
    grad_residual = grad_out + norm_back(grad_input_two, normed_two, inverse_two, second_gain)
    grad_b_out = jnp.sum(grad_residual, 0)
    grad_res_own = grad_residual.astype(LOW)
    grad_res_other = swap(grad_res_own)

    grad_mix_own = dot_rows(grad_res_own, out_full).astype(LOW)
    grad_mix_other = dot_rows(grad_res_other, out_full).astype(LOW)
    grad_mix_own, grad_down_part, grad_up_part = lax.optimization_barrier(
        (grad_mix_own, grad_down_part, grad_up_part)
    )
    grad_down = scatter_rows(grad_down_part)
    grad_up = scatter_rows(grad_up_part)
    dqkv_own, dqkv_other = attention_back(
        valid_both[:, :, None], qkv_own, qkv_other, grad_mix_own, grad_mix_other
    )
    input_other_part = swap(dot_last(dqkv_other, qkv_full).astype(LOW))
    input_own_part = dot_last(dqkv_own, qkv_full)
    grad_qkv = dot_first(
        jnp.concatenate([input_own, input_other], 0), jnp.concatenate([dqkv_own, dqkv_other], 0)
    )
    grad_out_weight = dot_first(
        jnp.concatenate([grad_res_own, grad_res_other], 0),
        jnp.concatenate(mix_own + mix_other, 0),
    )
    tail = scatter_rows(
        jnp.concatenate(
            [pad_cols(grad_qkv.astype(LOW), lane_qkv), grad_out_weight.astype(LOW)], 1
        )
    )
    bias_sums = jnp.sum(dqkv_own.astype(jnp.float32), 0) + jnp.sum(
        dqkv_other.astype(jnp.float32), 0
    )
    grad_input_one = input_own_part + input_other_part.astype(jnp.float32)
    grad_first_gain = jnp.sum(grad_input_one * normed_one, 0)
    grad_first_shift = jnp.sum(grad_input_one, 0)
    grad_activations = grad_residual + norm_back(
        grad_input_one, normed_one, inverse_one, first_gain
    )
    sums = lax.psum(
        (
            grad_first_gain,
            grad_first_shift,
            widen(bias_sums[:cols], b_query.shape[0], mp_index),
            widen(bias_sums[2 * cols :], b_value.shape[0], mp_index),
            grad_b_out,
            grad_second_gain,
            grad_second_shift,
            widen(grad_b_up_here, b_up.shape[0], mp_index),
            grad_b_down,
        ),
        ("dp", "mp"),
    )
    return (
        output.reshape(activations.shape),
        grad_activations.reshape(activations.shape),
        sums[0],
        sums[1],
        tail[:, :cols],
        sums[2],
        tail[:, cols : 2 * cols],
        tail[:, 2 * cols : 3 * cols],
        sums[3],
        tail[:, lane_qkv:].T,
        sums[4],
        sums[5],
        sums[6],
        grad_up,
        sums[7],
        grad_down.T,
        sums[8],
    )


def solution(mesh):
    two_way = mesh.shape["mp"] == 2
    step = jax.shard_map(
        local_pair if two_way else local,
        mesh=mesh,
        in_specs=(
            P("dp", "mp", None),
            P("dp", None),
            P(),
            P(),
            P("dp", "mp"),
            P(),
            P("dp", "mp"),
            P("dp", "mp"),
            P(),
            P("mp", "dp"),
            P(),
            P(),
            P(),
            P("dp", "mp"),
            P(),
            P("mp", "dp"),
            P(),
            P("dp", "mp", None),
        ),
        out_specs=(
            P("dp", "mp", None),
            P("dp", "mp", None),
            P(),
            P(),
            P("dp", "mp"),
            P(),
            P("dp", "mp"),
            P("dp", "mp"),
            P(),
            P("mp", "dp"),
            P(),
            P(),
            P(),
            P("dp", "mp"),
            P(),
            P("mp", "dp"),
            P(),
        ),
        check_vma=False,
    )
    return step
```

```python
import functools

import jax
import jax.numpy as jnp
from jax import lax
from jax.experimental import pallas as pl
from jax.experimental.layout import Layout, with_layout_constraint
from jax.sharding import PartitionSpec as P

HEAD_DIM = 72


EPS = 1e-06


def normalize(tensor):
    average = jnp.mean(tensor, -1, keepdims=True)
    centred = tensor - average
    spread = jnp.mean(centred * centred, -1, keepdims=True)
    inverse = lax.rsqrt(spread + EPS)
    return (centred * inverse, inverse)


def norm_back(grad_norm, normed, inverse, norm_gain):
    scaled = grad_norm * norm_gain
    first_mean = jnp.mean(scaled, -1, keepdims=True)
    second_mean = jnp.mean(scaled * normed, -1, keepdims=True)
    return inverse * (scaled - first_mean - normed * second_mean)


def flat_rows(tensor):
    return tensor.reshape(-1, tensor.shape[-1])


def right_dot(left_side, right_side):
    return jnp.dot(flat_rows(left_side), right_side, preferred_element_type=jnp.float32)


def inner_dot(left_side, right_side):
    return lax.dot_general(
        flat_rows(left_side),
        flat_rows(right_side),
        (((0,), (0,)), ((), ())),
        preferred_element_type=jnp.float32,
    )


def transposed_dot(left_side, right_side):
    return lax.dot_general(
        flat_rows(left_side),
        right_side,
        (((1,), (1,)), ((), ())),
        preferred_element_type=jnp.float32,
    )


def activate(hidden):
    return jax.nn.gelu(hidden, approximate=True)


def collect(tensor):
    return lax.all_gather(tensor, "mp", axis=1, tiled=True)


def collect_again(tensor):
    return lax.all_gather(tensor, "mp", axis=1, tiled=True)


def spread_sum(tensor):
    return lax.psum_scatter(
        tensor.astype(jnp.bfloat16), "mp", scatter_dimension=1, tiled=True
    ).astype(jnp.float32)


def widen(vector, length, mp_index):
    return lax.dynamic_update_slice_in_dim(
        jnp.zeros((length,), jnp.float32), vector, mp_index * vector.shape[0], 0
    )


def project(rows, query_full, key_full, value_full, query_bias, value_bias):
    shape = rows.shape[:2] + (query_full.shape[1],)
    queries = (right_dot(rows, query_full) + query_bias).astype(jnp.bfloat16).reshape(shape)
    key_rows = right_dot(rows, key_full).astype(jnp.bfloat16).reshape(shape)
    values = (right_dot(rows, value_full) + value_bias).astype(jnp.bfloat16).reshape(shape)
    return (queries, key_rows, values)


def expand(rows, up_full, up_bias):
    hidden = right_dot(rows, up_full) + up_bias
    return (hidden, activate(hidden).astype(jnp.bfloat16))


def split_heads(tensor):
    return tensor.reshape(tensor.shape[0], tensor.shape[1] // HEAD_DIM, HEAD_DIM)


def scores_of(queries, key_rows):
    raw_scores = jnp.einsum(
        "qhd,khd->hqk",
        split_heads(queries),
        split_heads(key_rows),
        preferred_element_type=jnp.float32,
    )
    return raw_scores * HEAD_DIM ** (-0.5)


def attend_forward(image_block):
    queries, key_rows, values, validity = image_block
    unnorm = validity[None, None, :] * jnp.exp(scores_of(queries, key_rows))
    row_total = jnp.maximum(jnp.sum(unnorm, -1, keepdims=True), 1.0)
    attention = (unnorm / row_total).astype(jnp.bfloat16)
    mixture = jnp.einsum(
        "hqk,khd->qhd", attention, split_heads(values), preferred_element_type=jnp.float32
    )
    return (mixture.reshape(queries.shape).astype(jnp.bfloat16), jnp.log(row_total))


def attend_back(image_block):
    queries, key_rows, values, validity, log_total, grad_mixture = image_block
    attention = validity[None, None, :] * jnp.exp(scores_of(queries, key_rows) - log_total)
    bound = (log_total > 0.0).astype(jnp.float32)
    grad_heads = split_heads(grad_mixture)
    grad_attention = jnp.einsum(
        "qhd,khd->hqk", grad_heads, split_heads(values), preferred_element_type=jnp.float32
    )
    row_delta = bound * jnp.sum(attention * grad_attention, -1, keepdims=True)
    grad_scores = (attention * (grad_attention - row_delta) * HEAD_DIM ** (-0.5)).astype(
        jnp.bfloat16
    )
    grad_queries = jnp.einsum(
        "hqk,khd->qhd", grad_scores, split_heads(key_rows), preferred_element_type=jnp.float32
    )
    grad_keys = jnp.einsum(
        "hqk,qhd->khd", grad_scores, split_heads(queries), preferred_element_type=jnp.float32
    )
    grad_values = jnp.einsum(
        "hqk,qhd->khd",
        attention.astype(jnp.bfloat16),
        grad_heads,
        preferred_element_type=jnp.float32,
    )
    shape = queries.shape
    return (
        grad_queries.reshape(shape).astype(jnp.bfloat16),
        grad_keys.reshape(shape).astype(jnp.bfloat16),
        grad_values.reshape(shape).astype(jnp.bfloat16),
    )


def local(
    activations,
    valid_mask,
    first_gain,
    first_shift,
    w_query,
    b_query,
    w_key,
    w_value,
    b_value,
    w_out,
    b_out,
    second_gain,
    second_shift,
    w_up,
    b_up,
    w_down,
    b_down,
    cotangent,
):
    images, local_rows, width = activations.shape
    mp_index = lax.axis_index("mp")
    head_cols = w_query.shape[1]
    hidden_cols = w_up.shape[1]
    validity = valid_mask.astype(jnp.float32)
    row_valid = lax.dynamic_slice_in_dim(validity, mp_index * local_rows, local_rows, 1)
    query_bias = lax.dynamic_slice_in_dim(b_query, mp_index * head_cols, head_cols)
    value_bias = lax.dynamic_slice_in_dim(b_value, mp_index * head_cols, head_cols)
    up_bias = lax.dynamic_slice_in_dim(b_up, mp_index * hidden_cols, hidden_cols)
    low_type = jnp.bfloat16
    normed_one, inverse_one = normalize(activations)
    input_one = (normed_one * first_gain + first_shift).astype(low_type)
    query_full, key_full, value_full, out_full = (
        lax.all_gather(w_query.astype(low_type), "dp", axis=0, tiled=True),
        lax.all_gather(w_key.astype(low_type), "dp", axis=0, tiled=True),
        lax.all_gather(w_value.astype(low_type), "dp", axis=0, tiled=True),
        lax.all_gather(w_out.astype(low_type), "dp", axis=1, tiled=True),
    )
    rows_one = collect(input_one)
    queries, key_rows, values = project(
        rows_one, query_full, key_full, value_full, query_bias, value_bias
    )
    mixture, log_total = lax.map(attend_forward, (queries, key_rows, values, validity))
    attn_part = right_dot(mixture, out_full).reshape(rows_one.shape)
    residual = activations + spread_sum(attn_part) + b_out
    normed_two, inverse_two = normalize(residual)
    input_two = (normed_two * second_gain + second_shift).astype(low_type)
    up_full, down_full = (
        lax.all_gather(w_up.astype(low_type), "dp", axis=0, tiled=True),
        lax.all_gather(w_down.astype(low_type), "dp", axis=1, tiled=True),
    )
    rows_two = collect(input_two)
    hidden, active = expand(rows_two, up_full, up_bias)
    mlp_part = jnp.dot(active, down_full, preferred_element_type=jnp.float32).reshape(
        rows_two.shape
    )
    output = residual + spread_sum(mlp_part) + b_down
    grad_out = cotangent * row_valid[:, :, None]
    grad_b_down = jnp.sum(grad_out, (0, 1))
    grad_rows_two = collect(grad_out.astype(low_type))
    up_back, down_back = (
        lax.all_gather(w_up.astype(low_type), "dp", axis=0, tiled=True),
        lax.all_gather(w_down.astype(low_type), "dp", axis=1, tiled=True),
    )
    rows_two_back = collect_again(input_two)
    hidden_back, active_back = expand(rows_two_back, up_back, up_bias)
    grad_w_down = inner_dot(active_back, grad_rows_two)
    grad_active = transposed_dot(grad_rows_two, down_back)
    grad_hidden = jax.vjp(activate, hidden_back)[1](grad_active)[0].astype(low_type)
    grad_b_up_here = jnp.sum(grad_hidden.astype(jnp.float32), 0)
    grad_w_up = inner_dot(rows_two_back, grad_hidden)
    grad_input_two = spread_sum(transposed_dot(grad_hidden, up_back).reshape(rows_two.shape))
    grad_second_gain = jnp.sum(grad_input_two * normed_two, (0, 1))
    grad_second_shift = jnp.sum(grad_input_two, (0, 1))
    grad_residual = grad_out + norm_back(grad_input_two, normed_two, inverse_two, second_gain)
    grad_b_out = jnp.sum(grad_residual, (0, 1))
    grad_rows_one = collect(grad_residual.astype(low_type))
    query_back, key_back, value_back, out_back = (
        lax.all_gather(w_query.astype(low_type), "dp", axis=0, tiled=True),
        lax.all_gather(w_key.astype(low_type), "dp", axis=0, tiled=True),
        lax.all_gather(w_value.astype(low_type), "dp", axis=0, tiled=True),
        lax.all_gather(w_out.astype(low_type), "dp", axis=1, tiled=True),
    )
    rows_one_back = collect_again(input_one)
    queries_back, key_rows_back, values_back = project(
        rows_one_back, query_back, key_back, value_back, query_bias, value_bias
    )
    mixture_back, log_total_back = lax.map(
        attend_forward, (queries_back, key_rows_back, values_back, validity)
    )
    grad_w_out = inner_dot(mixture_back, grad_rows_one)
    grad_mixture = (
        transposed_dot(grad_rows_one, out_back).astype(low_type).reshape(queries_back.shape)
    )
    grad_queries, grad_keys, grad_values = lax.map(
        attend_back,
        (queries_back, key_rows_back, values_back, validity, log_total_back, grad_mixture),
    )
    grad_w_query = inner_dot(rows_one_back, grad_queries)
    grad_w_key = inner_dot(rows_one_back, grad_keys)
    grad_w_value = inner_dot(rows_one_back, grad_values)
    grad_b_query_here = jnp.sum(grad_queries.astype(jnp.float32), (0, 1))
    grad_b_value_here = jnp.sum(grad_values.astype(jnp.float32), (0, 1))
    grad_input_part = (
        transposed_dot(grad_queries, query_back)
        + transposed_dot(grad_keys, key_back)
        + transposed_dot(grad_values, value_back)
    )
    grad_input_one = spread_sum(grad_input_part.reshape(rows_one.shape))
    grad_first_gain = jnp.sum(grad_input_one * normed_one, (0, 1))
    grad_first_shift = jnp.sum(grad_input_one, (0, 1))
    grad_activations = grad_residual + norm_back(
        grad_input_one, normed_one, inverse_one, first_gain
    )
    (
        grad_w_query_shard,
        grad_w_key_shard,
        grad_w_value_shard,
        grad_w_out_shard,
        grad_w_up_shard,
        grad_w_down_shard,
    ) = (
        lax.psum_scatter(
            grad_w_query.astype(jnp.bfloat16), "dp", scatter_dimension=0, tiled=True
        ).astype(jnp.float32),
        lax.psum_scatter(
            grad_w_key.astype(jnp.bfloat16), "dp", scatter_dimension=0, tiled=True
        ).astype(jnp.float32),
        lax.psum_scatter(
            grad_w_value.astype(jnp.bfloat16), "dp", scatter_dimension=0, tiled=True
        ).astype(jnp.float32),
        lax.psum_scatter(
            grad_w_out.astype(jnp.bfloat16), "dp", scatter_dimension=1, tiled=True
        ).astype(jnp.float32),
        lax.psum_scatter(
            grad_w_up.astype(jnp.bfloat16), "dp", scatter_dimension=0, tiled=True
        ).astype(jnp.float32),
        lax.psum_scatter(
            grad_w_down.astype(jnp.bfloat16), "dp", scatter_dimension=1, tiled=True
        ).astype(jnp.float32),
    )
    vector_sums = lax.psum(
        (
            grad_first_gain,
            grad_first_shift,
            widen(grad_b_query_here, b_query.shape[0], mp_index),
            widen(grad_b_value_here, b_value.shape[0], mp_index),
            grad_b_out,
            grad_second_gain,
            grad_second_shift,
            widen(grad_b_up_here, b_up.shape[0], mp_index),
            grad_b_down,
        ),
        ("dp", "mp"),
    )
    return (
        output,
        grad_activations,
        vector_sums[0],
        vector_sums[1],
        grad_w_query_shard,
        vector_sums[2],
        grad_w_key_shard,
        grad_w_value_shard,
        vector_sums[3],
        grad_w_out_shard,
        vector_sums[4],
        vector_sums[5],
        vector_sums[6],
        grad_w_up_shard,
        vector_sums[7],
        grad_w_down_shard,
        vector_sums[8],
    )


SCALE = HEAD_DIM ** (-0.5)
LOW = jnp.bfloat16


def swap(tensor):
    return lax.ppermute(tensor, "mp", [(0, 1), (1, 0)])


def dot_rows(left_side, right_side):
    return lax.dot_general(
        left_side, right_side, (((1,), (0,)), ((), ())), preferred_element_type=jnp.float32
    )


def dot_last(left_side, right_side):
    return lax.dot_general(
        left_side, right_side, (((1,), (1,)), ((), ())), preferred_element_type=jnp.float32
    )


def dot_first(left_side, right_side):
    return lax.dot_general(
        left_side, right_side, (((0,), (0,)), ((), ())), preferred_element_type=jnp.float32
    )


def attention_kernel(valid_ref, own_ref, other_ref, mix_own_ref, mix_other_ref):
    width = mix_own_ref.shape[1]
    valid = valid_ref[0]
    for head in range(width // HEAD_DIM):
        cols = slice(head * HEAD_DIM, (head + 1) * HEAD_DIM)
        key_cols = slice(width + head * HEAD_DIM, width + (head + 1) * HEAD_DIM)
        value_cols = slice(2 * width + head * HEAD_DIM, 2 * width + (head + 1) * HEAD_DIM)
        keys = jnp.concatenate([own_ref[:, key_cols], other_ref[:, key_cols]], 0)
        values = jnp.concatenate([own_ref[:, value_cols], other_ref[:, value_cols]], 0)
        for source, target in ((own_ref, mix_own_ref), (other_ref, mix_other_ref)):
            unnorm = jnp.exp(dot_last(source[:, cols], keys) * SCALE) * valid
            row_total = jnp.maximum(jnp.sum(unnorm, -1, keepdims=True), 1.0)
            attention = (unnorm * (1.0 / row_total)).astype(LOW)
            target[:, cols] = dot_rows(attention, values).astype(LOW)


def attention_cost(rows, width, dots):
    heads = width // HEAD_DIM
    return pl.CostEstimate(
        flops=dots * heads * 2 * 4 * rows * rows * 256,
        transcendentals=heads * 4 * rows * rows,
        bytes_accessed=20 * rows * width,
    )


def attention_forward(valid_rows, own, other, image, width):
    rows = own.shape[0] // valid_rows.shape[0]
    block = pl.BlockSpec((rows, own.shape[1]), lambda step: (image, 0))
    mix_block = pl.BlockSpec((rows, width), lambda step: (0, 0))
    mix_shape = jax.ShapeDtypeStruct((rows, width), LOW)
    return pl.pallas_call(
        attention_kernel,
        grid=(1,),
        in_specs=[pl.BlockSpec((1, 1, 2 * rows), lambda step: (image, 0, 0)), block, block],
        out_specs=[mix_block, mix_block],
        out_shape=[mix_shape, mix_shape],
        cost_estimate=attention_cost(rows, width, 2),
        name="attention_forward",
    )(valid_rows, own, other)


def attention_back_kernel(
    valid_ref, own_ref, other_ref, grad_own_ref, grad_other_ref, out_own_ref, out_other_ref
):
    rows, width = grad_own_ref.shape
    valid = valid_ref[0]
    for head in range(width // HEAD_DIM):
        cols = slice(head * HEAD_DIM, (head + 1) * HEAD_DIM)
        key_cols = slice(width + head * HEAD_DIM, width + (head + 1) * HEAD_DIM)
        value_cols = slice(2 * width + head * HEAD_DIM, 2 * width + (head + 1) * HEAD_DIM)
        keys = jnp.concatenate([own_ref[:, key_cols], other_ref[:, key_cols]], 0)
        values = jnp.concatenate([own_ref[:, value_cols], other_ref[:, value_cols]], 0)
        keys_turned = keys.T
        grad_keys = None
        grad_values = None
        for source, grad_source, target in (
            (own_ref, grad_own_ref, out_own_ref),
            (other_ref, grad_other_ref, out_other_ref),
        ):
            queries = source[:, cols]
            grad_mix = grad_source[:, cols]
            unnorm = jnp.exp(dot_last(keys, queries) * SCALE) * valid
            row_total = jnp.maximum(jnp.sum(unnorm, 0, keepdims=True), 1.0)
            attention = unnorm * (1.0 / row_total)
            bound = jnp.where(row_total > 1.0, 1.0, 0.0)
            grad_attention = dot_last(values, grad_mix)
            row_delta = bound * jnp.sum(attention * grad_attention, 0, keepdims=True)
            grad_scores = (attention * (grad_attention - row_delta) * SCALE).astype(LOW)
            grad_turned = dot_rows(keys_turned, grad_scores)
            target[:, cols] = grad_turned.T.astype(LOW)
            add_keys = dot_rows(grad_scores, queries)
            add_values = dot_rows(attention.astype(LOW), grad_mix)
            grad_keys = add_keys if grad_keys is None else grad_keys + add_keys
            grad_values = add_values if grad_values is None else grad_values + add_values
        grad_keys = grad_keys.astype(LOW)
        grad_values = grad_values.astype(LOW)
        out_own_ref[:, key_cols] = grad_keys[:rows]
        out_other_ref[:, key_cols] = grad_keys[rows:]
        out_own_ref[:, value_cols] = grad_values[:rows]
        out_other_ref[:, value_cols] = grad_values[rows:]


def attention_back(valid_cols, own, other, grad_own, grad_other):
    images = valid_cols.shape[0]
    rows = own.shape[0] // images
    block = pl.BlockSpec((rows, own.shape[1]), lambda step: (step, 0))
    grad_block = pl.BlockSpec((rows, grad_own.shape[1]), lambda step: (step, 0))
    out_shape = jax.ShapeDtypeStruct(own.shape, LOW)
    return pl.pallas_call(
        attention_back_kernel,
        grid=(images,),
        in_specs=[
            pl.BlockSpec((1, 2 * rows, 1), lambda step: (step, 0, 0)),
            block,
            block,
            grad_block,
            grad_block,
        ],
        out_specs=[block, block],
        out_shape=[out_shape, out_shape],
        cost_estimate=attention_cost(rows, grad_own.shape[1], 5 * images),
        name="attention_back",
    )(valid_cols, own, other, grad_own, grad_other)


def weight_grad_kernel(layout, *refs):
    out_ref = refs[-1]
    position = 0
    filled = 0
    for chunks, start, cols in layout:
        total = None
        for _ in range(chunks):
            part = dot_first(refs[position][...], refs[position + 1][...])
            total = part if total is None else total + part
            position += 2
        if start > filled:
            out_ref[:, filled:start] = jnp.zeros((out_ref.shape[0], start - filled), LOW)
        out_ref[:, start : start + cols] = total.astype(LOW)
        filled = start + cols


def weight_grads(sections, name):
    width = sections[0][0][0].shape[1]
    block_rows = width // 3
    layout, operands, specs = [], [], []
    start, flops = 0, 0
    for pairs in sections:
        cols = pairs[0][1].shape[1]
        start = -(-start // 128) * 128
        layout.append((len(pairs), start, cols))
        start += cols
        for left_side, right_side in pairs:
            operands += [left_side, right_side]
            flops += 2 * left_side.shape[0] * width * cols
            specs += [
                pl.BlockSpec((left_side.shape[0], block_rows), lambda step: (0, step)),
                pl.BlockSpec(
                    right_side.shape, lambda step: (0, 0), pipeline_mode=pl.Buffered(1)
                ),
            ]
    moved = sum(2 * operand.size for operand in operands) + 2 * width * start
    return pl.pallas_call(
        functools.partial(weight_grad_kernel, tuple(layout)),
        grid=(3,),
        in_specs=specs,
        out_specs=pl.BlockSpec((block_rows, start), lambda step: (step, 0)),
        out_shape=jax.ShapeDtypeStruct((width, start), LOW),
        cost_estimate=pl.CostEstimate(flops=flops, transcendentals=0, bytes_accessed=moved),
        name=name,
    )(*operands)


def sum_everywhere(vector):
    total = vector + swap(vector)
    devices = lax.axis_size("dp")
    step = 1
    while step < devices:
        pairs = [(index, index ^ step) for index in range(devices)]
        total = total + lax.ppermute(total, "dp", pairs)
        step *= 2
    return total


def pad_cols(tensor, width):
    return jnp.pad(tensor, ((0, 0), (0, width - tensor.shape[1])))


def gather_rows(tensor):
    return lax.all_gather(tensor, "dp", axis=0, tiled=True)


def scatter_rows(tensor):
    tensor = with_layout_constraint(tensor, Layout((0, 1)))
    part = lax.psum_scatter(tensor, "dp", scatter_dimension=0, tiled=True)
    return with_layout_constraint(part, Layout((0, 1))).astype(jnp.float32)


def local_pair(
    activations,
    valid_mask,
    first_gain,
    first_shift,
    w_query,
    b_query,
    w_key,
    w_value,
    b_value,
    w_out,
    b_out,
    second_gain,
    second_shift,
    w_up,
    b_up,
    w_down,
    b_down,
    cotangent,
):
    images, half, width = activations.shape
    mp_index = lax.axis_index("mp")
    cols = w_query.shape[1]
    units = w_up.shape[1]
    lane_units = -(-units // 128) * 128
    lane_qkv = -(-3 * cols // 128) * 128
    tokens = images * half
    validity = valid_mask.astype(jnp.float32)
    valid_own = lax.dynamic_slice_in_dim(validity, mp_index * half, half, 1)
    valid_other = lax.dynamic_slice_in_dim(validity, (1 - mp_index) * half, half, 1)
    valid_both = jnp.concatenate([valid_own, valid_other], 1)
    query_bias = lax.dynamic_slice_in_dim(b_query, mp_index * cols, cols)
    value_bias = lax.dynamic_slice_in_dim(b_value, mp_index * cols, cols)
    up_bias = lax.dynamic_slice_in_dim(b_up, mp_index * units, units)
    qkv_bias = jnp.concatenate([query_bias, jnp.zeros_like(query_bias), value_bias])

    qkv_shard = jnp.concatenate([w_query, w_key, w_value], 1).astype(LOW)
    first_full = gather_rows(
        jnp.concatenate([pad_cols(qkv_shard, lane_qkv), w_out.T.astype(LOW)], 1)
    )
    qkv_full = first_full[:, : 3 * cols]
    out_full = first_full[:, lane_qkv:]
    second_full = gather_rows(
        jnp.concatenate(
            [pad_cols(w_up.astype(LOW), lane_units), w_down.T.astype(LOW)], 1
        )
    )
    up_full = second_full[:, :units]
    down_full = second_full[:, lane_units:]

    flat = activations.reshape(tokens, width)
    normed_one, inverse_one = normalize(flat)
    input_own = (normed_one * first_gain + first_shift).astype(LOW)
    input_other = swap(input_own)
    grad_out = (cotangent * valid_own[:, :, None]).reshape(tokens, width)
    grad_b_down = jnp.sum(grad_out, 0)
    grad_rows_own = grad_out.astype(LOW)
    grad_rows_other = swap(grad_rows_own)

    qkv_own = (dot_rows(input_own, qkv_full) + qkv_bias).astype(LOW)
    qkv_other = (dot_rows(input_other, qkv_full) + qkv_bias).astype(LOW)

    mix_own, mix_other, residuals, normeds, inverses, lows, crossed = [], [], [], [], [], [], []
    for image in range(images):
        own, other = attention_forward(valid_both[:, None, :], qkv_own, qkv_other, image, cols)
        if image == 0:
            other, grad_rows_other = lax.optimization_barrier((other, grad_rows_other))
        mix_own.append(own)
        mix_other.append(other)
        received = swap(dot_last(other, out_full).astype(LOW))
        own_part = dot_last(own, out_full)
        if image > 0:
            received, own_part, lows[-1] = lax.optimization_barrier(
                (received, own_part, lows[-1])
            )
        residual = activations[image] + (own_part + received.astype(jnp.float32)) + b_out
        normed, inverse = normalize(residual)
        low_rows = (normed * second_gain + second_shift).astype(LOW)
        residuals.append(residual)
        normeds.append(normed)
        inverses.append(inverse)
        lows.append(low_rows)
        crossed.append(swap(low_rows))
    residual = jnp.concatenate(residuals, 0)
    normed_two = jnp.concatenate(normeds, 0)
    inverse_two = jnp.concatenate(inverses, 0)
    rows_own = jnp.concatenate(lows, 0)
    rows_other = jnp.concatenate(crossed, 0)

    hidden_own = dot_rows(rows_own, up_full) + up_bias
    active_own = activate(hidden_own).astype(LOW)
    hidden_other = dot_rows(rows_other, up_full) + up_bias
    active_other = activate(hidden_other).astype(LOW)

    grad_active = dot_rows(grad_rows_other, down_full)
    grad_hidden_other = jax.vjp(activate, hidden_other)[1](grad_active)[0].astype(LOW)
    back_other = swap(dot_last(grad_hidden_other, up_full).astype(LOW))
    grad_active = dot_rows(grad_rows_own, down_full)
    grad_hidden_own = jax.vjp(activate, hidden_own)[1](grad_active)[0].astype(LOW)
    back_own = dot_last(grad_hidden_own, up_full)
    grad_b_up_here = jnp.sum(grad_hidden_own.astype(jnp.float32), 0) + jnp.sum(
        grad_hidden_other.astype(jnp.float32), 0
    )
    wide_pack = weight_grads(
        (
            ((rows_own, grad_hidden_own), (rows_other, grad_hidden_other)),
            ((grad_rows_own, active_own), (grad_rows_other, active_other)),
        ),
        "wide_grads",
    )
    back_other, wide_pack = lax.optimization_barrier((back_other, wide_pack))
    wide = scatter_rows(wide_pack)

    mlp_other = dot_last(active_other, down_full).astype(LOW)
    mlp_own = dot_last(active_own, down_full)

    grad_input_two = back_own + back_other.astype(jnp.float32)
    grad_second_gain = jnp.sum(grad_input_two * normed_two, 0)
    grad_second_shift = jnp.sum(grad_input_two, 0)
    grad_residual = grad_out + norm_back(grad_input_two, normed_two, inverse_two, second_gain)
    grad_b_out = jnp.sum(grad_residual, 0)
    grad_res_own = grad_residual.astype(LOW)
    grad_res_other, mlp_other, mlp_own = lax.optimization_barrier(
        (swap(grad_res_own), mlp_other, mlp_own)
    )
    mlp_other = swap(mlp_other)

    grad_mix_own = dot_rows(grad_res_own, out_full).astype(LOW)
    grad_mix_other = dot_rows(grad_res_other, out_full).astype(LOW)
    dqkv_own, dqkv_other = attention_back(
        valid_both[:, :, None], qkv_own, qkv_other, grad_mix_own, grad_mix_other
    )
    tail_pack = weight_grads(
        (
            ((input_own, dqkv_own), (input_other, dqkv_other)),
            (
                (grad_res_own, jnp.concatenate(mix_own, 0)),
                (grad_res_other, jnp.concatenate(mix_other, 0)),
            ),
        ),
        "tail_grads",
    )
    dqkv_own, dqkv_other, tail_pack, mlp_other = lax.optimization_barrier(
        (dqkv_own, dqkv_other, tail_pack, mlp_other)
    )
    output = residual + (mlp_own + mlp_other.astype(jnp.float32)) + b_down
    tail_pack, wide = lax.optimization_barrier((tail_pack, wide))
    tail = scatter_rows(tail_pack)
    input_other_part = swap(dot_last(dqkv_other, qkv_full).astype(LOW))
    input_own_part = dot_last(dqkv_own, qkv_full)
    bias_sums = jnp.sum(dqkv_own.astype(jnp.float32), 0) + jnp.sum(
        dqkv_other.astype(jnp.float32), 0
    )
    grad_input_one = input_own_part + input_other_part.astype(jnp.float32)
    grad_first_gain = jnp.sum(grad_input_one * normed_one, 0)
    grad_first_shift = jnp.sum(grad_input_one, 0)
    grad_activations = grad_residual + norm_back(
        grad_input_one, normed_one, inverse_one, first_gain
    )
    vectors = (
        grad_first_gain,
        grad_first_shift,
        widen(bias_sums[:cols], b_query.shape[0], mp_index),
        widen(bias_sums[2 * cols :], b_value.shape[0], mp_index),
        grad_b_out,
        grad_second_gain,
        grad_second_shift,
        widen(grad_b_up_here, b_up.shape[0], mp_index),
        grad_b_down,
    )
    packed = jnp.concatenate(vectors)
    lanes = -(-packed.shape[0] // 1024) * 1024
    packed = jnp.pad(packed, (0, lanes - packed.shape[0])).reshape(-1, 128)
    packed = sum_everywhere(packed).reshape(-1)
    sums, place = [], 0
    for vector in vectors:
        sums.append(packed[place : place + vector.shape[0]])
        place += vector.shape[0]
    return (
        output.reshape(activations.shape),
        grad_activations.reshape(activations.shape),
        sums[0],
        sums[1],
        tail[:, :cols],
        sums[2],
        tail[:, cols : 2 * cols],
        tail[:, 2 * cols : 3 * cols],
        sums[3],
        tail[:, lane_qkv:].T,
        sums[4],
        sums[5],
        sums[6],
        wide[:, :units],
        sums[7],
        wide[:, lane_units:].T,
        sums[8],
    )


def solution(mesh):
    two_way = mesh.shape["mp"] == 2 and mesh.shape["dp"] & (mesh.shape["dp"] - 1) == 0
    step = jax.shard_map(
        local_pair if two_way else local,
        mesh=mesh,
        in_specs=(
            P("dp", "mp", None),
            P("dp", None),
            P(),
            P(),
            P("dp", "mp"),
            P(),
            P("dp", "mp"),
            P("dp", "mp"),
            P(),
            P("mp", "dp"),
            P(),
            P(),
            P(),
            P("dp", "mp"),
            P(),
            P("mp", "dp"),
            P(),
            P("dp", "mp", None),
        ),
        out_specs=(
            P("dp", "mp", None),
            P("dp", "mp", None),
            P(),
            P(),
            P("dp", "mp"),
            P(),
            P("dp", "mp"),
            P("dp", "mp"),
            P(),
            P("mp", "dp"),
            P(),
            P(),
            P(),
            P("dp", "mp"),
            P(),
            P("mp", "dp"),
            P(),
        ),
        check_vma=False,
    )
    return step
```

```python
import functools
import math

import jax
import jax.numpy as jnp
from jax import lax
from jax.experimental import pallas as pl
from jax.experimental.layout import Layout, with_layout_constraint
from jax.sharding import PartitionSpec as P

HEAD_DIM = 72


EPS = 1e-06


def normalize(tensor):
    average = jnp.mean(tensor, -1, keepdims=True)
    centred = tensor - average
    spread = jnp.mean(centred * centred, -1, keepdims=True)
    inverse = lax.rsqrt(spread + EPS)
    return (centred * inverse, inverse)


def norm_back(grad_norm, normed, inverse, norm_gain):
    scaled = grad_norm * norm_gain
    first_mean = jnp.mean(scaled, -1, keepdims=True)
    second_mean = jnp.mean(scaled * normed, -1, keepdims=True)
    return inverse * (scaled - first_mean - normed * second_mean)


def flat_rows(tensor):
    return tensor.reshape(-1, tensor.shape[-1])


def right_dot(left_side, right_side):
    return jnp.dot(flat_rows(left_side), right_side, preferred_element_type=jnp.float32)


def inner_dot(left_side, right_side):
    return lax.dot_general(
        flat_rows(left_side),
        flat_rows(right_side),
        (((0,), (0,)), ((), ())),
        preferred_element_type=jnp.float32,
    )


def transposed_dot(left_side, right_side):
    return lax.dot_general(
        flat_rows(left_side),
        right_side,
        (((1,), (1,)), ((), ())),
        preferred_element_type=jnp.float32,
    )


def activate(hidden):
    return jax.nn.gelu(hidden, approximate=True)


def collect(tensor):
    return lax.all_gather(tensor, "mp", axis=1, tiled=True)


def collect_again(tensor):
    return lax.all_gather(tensor, "mp", axis=1, tiled=True)


def spread_sum(tensor):
    return lax.psum_scatter(
        tensor.astype(jnp.bfloat16), "mp", scatter_dimension=1, tiled=True
    ).astype(jnp.float32)


def widen(vector, length, mp_index):
    return lax.dynamic_update_slice_in_dim(
        jnp.zeros((length,), jnp.float32), vector, mp_index * vector.shape[0], 0
    )


def project(rows, query_full, key_full, value_full, query_bias, value_bias):
    shape = rows.shape[:2] + (query_full.shape[1],)
    queries = (right_dot(rows, query_full) + query_bias).astype(jnp.bfloat16).reshape(shape)
    key_rows = right_dot(rows, key_full).astype(jnp.bfloat16).reshape(shape)
    values = (right_dot(rows, value_full) + value_bias).astype(jnp.bfloat16).reshape(shape)
    return (queries, key_rows, values)


def expand(rows, up_full, up_bias):
    hidden = right_dot(rows, up_full) + up_bias
    return (hidden, activate(hidden).astype(jnp.bfloat16))


def split_heads(tensor):
    return tensor.reshape(tensor.shape[0], tensor.shape[1] // HEAD_DIM, HEAD_DIM)


def scores_of(queries, key_rows):
    raw_scores = jnp.einsum(
        "qhd,khd->hqk",
        split_heads(queries),
        split_heads(key_rows),
        preferred_element_type=jnp.float32,
    )
    return raw_scores * HEAD_DIM ** (-0.5)


def attend_forward(image_block):
    queries, key_rows, values, validity = image_block
    unnorm = validity[None, None, :] * jnp.exp(scores_of(queries, key_rows))
    row_total = jnp.maximum(jnp.sum(unnorm, -1, keepdims=True), 1.0)
    attention = (unnorm / row_total).astype(jnp.bfloat16)
    mixture = jnp.einsum(
        "hqk,khd->qhd", attention, split_heads(values), preferred_element_type=jnp.float32
    )
    return (mixture.reshape(queries.shape).astype(jnp.bfloat16), jnp.log(row_total))


def attend_back(image_block):
    queries, key_rows, values, validity, log_total, grad_mixture = image_block
    attention = validity[None, None, :] * jnp.exp(scores_of(queries, key_rows) - log_total)
    bound = (log_total > 0.0).astype(jnp.float32)
    grad_heads = split_heads(grad_mixture)
    grad_attention = jnp.einsum(
        "qhd,khd->hqk", grad_heads, split_heads(values), preferred_element_type=jnp.float32
    )
    row_delta = bound * jnp.sum(attention * grad_attention, -1, keepdims=True)
    grad_scores = (attention * (grad_attention - row_delta) * HEAD_DIM ** (-0.5)).astype(
        jnp.bfloat16
    )
    grad_queries = jnp.einsum(
        "hqk,khd->qhd", grad_scores, split_heads(key_rows), preferred_element_type=jnp.float32
    )
    grad_keys = jnp.einsum(
        "hqk,qhd->khd", grad_scores, split_heads(queries), preferred_element_type=jnp.float32
    )
    grad_values = jnp.einsum(
        "hqk,qhd->khd",
        attention.astype(jnp.bfloat16),
        grad_heads,
        preferred_element_type=jnp.float32,
    )
    shape = queries.shape
    return (
        grad_queries.reshape(shape).astype(jnp.bfloat16),
        grad_keys.reshape(shape).astype(jnp.bfloat16),
        grad_values.reshape(shape).astype(jnp.bfloat16),
    )


def local(
    activations,
    valid_mask,
    first_gain,
    first_shift,
    w_query,
    b_query,
    w_key,
    w_value,
    b_value,
    w_out,
    b_out,
    second_gain,
    second_shift,
    w_up,
    b_up,
    w_down,
    b_down,
    cotangent,
):
    images, local_rows, width = activations.shape
    mp_index = lax.axis_index("mp")
    head_cols = w_query.shape[1]
    hidden_cols = w_up.shape[1]
    validity = valid_mask.astype(jnp.float32)
    row_valid = lax.dynamic_slice_in_dim(validity, mp_index * local_rows, local_rows, 1)
    query_bias = lax.dynamic_slice_in_dim(b_query, mp_index * head_cols, head_cols)
    value_bias = lax.dynamic_slice_in_dim(b_value, mp_index * head_cols, head_cols)
    up_bias = lax.dynamic_slice_in_dim(b_up, mp_index * hidden_cols, hidden_cols)
    low_type = jnp.bfloat16
    normed_one, inverse_one = normalize(activations)
    input_one = (normed_one * first_gain + first_shift).astype(low_type)
    query_full, key_full, value_full, out_full = (
        lax.all_gather(w_query.astype(low_type), "dp", axis=0, tiled=True),
        lax.all_gather(w_key.astype(low_type), "dp", axis=0, tiled=True),
        lax.all_gather(w_value.astype(low_type), "dp", axis=0, tiled=True),
        lax.all_gather(w_out.astype(low_type), "dp", axis=1, tiled=True),
    )
    rows_one = collect(input_one)
    queries, key_rows, values = project(
        rows_one, query_full, key_full, value_full, query_bias, value_bias
    )
    mixture, log_total = lax.map(attend_forward, (queries, key_rows, values, validity))
    attn_part = right_dot(mixture, out_full).reshape(rows_one.shape)
    residual = activations + spread_sum(attn_part) + b_out
    normed_two, inverse_two = normalize(residual)
    input_two = (normed_two * second_gain + second_shift).astype(low_type)
    up_full, down_full = (
        lax.all_gather(w_up.astype(low_type), "dp", axis=0, tiled=True),
        lax.all_gather(w_down.astype(low_type), "dp", axis=1, tiled=True),
    )
    rows_two = collect(input_two)
    hidden, active = expand(rows_two, up_full, up_bias)
    mlp_part = jnp.dot(active, down_full, preferred_element_type=jnp.float32).reshape(
        rows_two.shape
    )
    output = residual + spread_sum(mlp_part) + b_down
    grad_out = cotangent * row_valid[:, :, None]
    grad_b_down = jnp.sum(grad_out, (0, 1))
    grad_rows_two = collect(grad_out.astype(low_type))
    up_back, down_back = (
        lax.all_gather(w_up.astype(low_type), "dp", axis=0, tiled=True),
        lax.all_gather(w_down.astype(low_type), "dp", axis=1, tiled=True),
    )
    rows_two_back = collect_again(input_two)
    hidden_back, active_back = expand(rows_two_back, up_back, up_bias)
    grad_w_down = inner_dot(active_back, grad_rows_two)
    grad_active = transposed_dot(grad_rows_two, down_back)
    grad_hidden = jax.vjp(activate, hidden_back)[1](grad_active)[0].astype(low_type)
    grad_b_up_here = jnp.sum(grad_hidden.astype(jnp.float32), 0)
    grad_w_up = inner_dot(rows_two_back, grad_hidden)
    grad_input_two = spread_sum(transposed_dot(grad_hidden, up_back).reshape(rows_two.shape))
    grad_second_gain = jnp.sum(grad_input_two * normed_two, (0, 1))
    grad_second_shift = jnp.sum(grad_input_two, (0, 1))
    grad_residual = grad_out + norm_back(grad_input_two, normed_two, inverse_two, second_gain)
    grad_b_out = jnp.sum(grad_residual, (0, 1))
    grad_rows_one = collect(grad_residual.astype(low_type))
    query_back, key_back, value_back, out_back = (
        lax.all_gather(w_query.astype(low_type), "dp", axis=0, tiled=True),
        lax.all_gather(w_key.astype(low_type), "dp", axis=0, tiled=True),
        lax.all_gather(w_value.astype(low_type), "dp", axis=0, tiled=True),
        lax.all_gather(w_out.astype(low_type), "dp", axis=1, tiled=True),
    )
    rows_one_back = collect_again(input_one)
    queries_back, key_rows_back, values_back = project(
        rows_one_back, query_back, key_back, value_back, query_bias, value_bias
    )
    mixture_back, log_total_back = lax.map(
        attend_forward, (queries_back, key_rows_back, values_back, validity)
    )
    grad_w_out = inner_dot(mixture_back, grad_rows_one)
    grad_mixture = (
        transposed_dot(grad_rows_one, out_back).astype(low_type).reshape(queries_back.shape)
    )
    grad_queries, grad_keys, grad_values = lax.map(
        attend_back,
        (queries_back, key_rows_back, values_back, validity, log_total_back, grad_mixture),
    )
    grad_w_query = inner_dot(rows_one_back, grad_queries)
    grad_w_key = inner_dot(rows_one_back, grad_keys)
    grad_w_value = inner_dot(rows_one_back, grad_values)
    grad_b_query_here = jnp.sum(grad_queries.astype(jnp.float32), (0, 1))
    grad_b_value_here = jnp.sum(grad_values.astype(jnp.float32), (0, 1))
    grad_input_part = (
        transposed_dot(grad_queries, query_back)
        + transposed_dot(grad_keys, key_back)
        + transposed_dot(grad_values, value_back)
    )
    grad_input_one = spread_sum(grad_input_part.reshape(rows_one.shape))
    grad_first_gain = jnp.sum(grad_input_one * normed_one, (0, 1))
    grad_first_shift = jnp.sum(grad_input_one, (0, 1))
    grad_activations = grad_residual + norm_back(
        grad_input_one, normed_one, inverse_one, first_gain
    )
    (
        grad_w_query_shard,
        grad_w_key_shard,
        grad_w_value_shard,
        grad_w_out_shard,
        grad_w_up_shard,
        grad_w_down_shard,
    ) = (
        lax.psum_scatter(
            grad_w_query.astype(jnp.bfloat16), "dp", scatter_dimension=0, tiled=True
        ).astype(jnp.float32),
        lax.psum_scatter(
            grad_w_key.astype(jnp.bfloat16), "dp", scatter_dimension=0, tiled=True
        ).astype(jnp.float32),
        lax.psum_scatter(
            grad_w_value.astype(jnp.bfloat16), "dp", scatter_dimension=0, tiled=True
        ).astype(jnp.float32),
        lax.psum_scatter(
            grad_w_out.astype(jnp.bfloat16), "dp", scatter_dimension=1, tiled=True
        ).astype(jnp.float32),
        lax.psum_scatter(
            grad_w_up.astype(jnp.bfloat16), "dp", scatter_dimension=0, tiled=True
        ).astype(jnp.float32),
        lax.psum_scatter(
            grad_w_down.astype(jnp.bfloat16), "dp", scatter_dimension=1, tiled=True
        ).astype(jnp.float32),
    )
    vector_sums = lax.psum(
        (
            grad_first_gain,
            grad_first_shift,
            widen(grad_b_query_here, b_query.shape[0], mp_index),
            widen(grad_b_value_here, b_value.shape[0], mp_index),
            grad_b_out,
            grad_second_gain,
            grad_second_shift,
            widen(grad_b_up_here, b_up.shape[0], mp_index),
            grad_b_down,
        ),
        ("dp", "mp"),
    )
    return (
        output,
        grad_activations,
        vector_sums[0],
        vector_sums[1],
        grad_w_query_shard,
        vector_sums[2],
        grad_w_key_shard,
        grad_w_value_shard,
        vector_sums[3],
        grad_w_out_shard,
        vector_sums[4],
        vector_sums[5],
        vector_sums[6],
        grad_w_up_shard,
        vector_sums[7],
        grad_w_down_shard,
        vector_sums[8],
    )


SCALE = HEAD_DIM ** (-0.5)
SCALE_TWO = SCALE / math.log(2.0)
LOW = jnp.bfloat16


def swap(tensor):
    return lax.ppermute(tensor, "mp", [(0, 1), (1, 0)])


def dot_rows(left_side, right_side):
    return lax.dot_general(
        left_side, right_side, (((1,), (0,)), ((), ())), preferred_element_type=jnp.float32
    )


def dot_last(left_side, right_side):
    return lax.dot_general(
        left_side, right_side, (((1,), (1,)), ((), ())), preferred_element_type=jnp.float32
    )


def dot_first(left_side, right_side):
    return lax.dot_general(
        left_side, right_side, (((0,), (0,)), ((), ())), preferred_element_type=jnp.float32
    )


def head_columns(ref, part, head, width):
    first = part * width + head * HEAD_DIM
    return ref[:, first : first + HEAD_DIM]


def attention_cost(rows, width, dots):
    heads = width // HEAD_DIM
    return pl.CostEstimate(
        flops=dots * heads * 2 * rows * rows * 256,
        transcendentals=heads * rows * rows,
        bytes_accessed=10 * rows * width,
    )


def attention_kernel(valid_ref, qkv_ref, mix_ref):
    rows, width = mix_ref.shape
    half = rows // 2
    valid = valid_ref[...]
    for head in range(width // HEAD_DIM):
        first = head * HEAD_DIM
        keys = head_columns(qkv_ref, 1, head, width)
        values = head_columns(qkv_ref, 2, head, width)
        for start in (0, half):
            queries = qkv_ref[start : start + half, first : first + HEAD_DIM]
            unnorm = jnp.exp2(dot_last(queries, keys) * SCALE_TWO) * valid
            row_total = jnp.maximum(jnp.sum(unnorm, -1, keepdims=True), 1.0)
            attention = (unnorm * (1.0 / row_total)).astype(LOW)
            mix_ref[start : start + half, first : first + HEAD_DIM] = dot_rows(
                attention, values
            ).astype(LOW)


def attention_forward(valid_row, qkv):
    rows, width = qkv.shape[0], qkv.shape[1] // 3
    return pl.pallas_call(
        attention_kernel,
        out_shape=jax.ShapeDtypeStruct((rows, width), LOW),
        cost_estimate=attention_cost(rows, width, 2),
        name="attention_forward",
    )(valid_row, qkv)


def attention_back_kernel(valid_ref, qkv_ref, grad_ref, out_ref):
    rows, width = grad_ref.shape
    half = rows // 2
    valid = valid_ref[...]
    for head in range(width // HEAD_DIM):
        first = head * HEAD_DIM
        keys = head_columns(qkv_ref, 1, head, width)
        values = head_columns(qkv_ref, 2, head, width)
        keys_turned = keys.T
        grad_keys = None
        grad_values = None
        for start in (0, half):
            queries = qkv_ref[start : start + half, first : first + HEAD_DIM]
            grad_mix = grad_ref[start : start + half, first : first + HEAD_DIM]
            unnorm = jnp.exp2(dot_last(keys, queries) * SCALE_TWO) * valid
            row_total = jnp.maximum(jnp.sum(unnorm, 0, keepdims=True), 1.0)
            attention = unnorm * (1.0 / row_total)
            bound = jnp.where(row_total > 1.0, 1.0, 0.0)
            grad_attention = dot_last(values, grad_mix)
            row_delta = bound * jnp.sum(attention * grad_attention, 0, keepdims=True)
            grad_scores = (attention * (grad_attention - row_delta)).astype(LOW)
            grad_turned = dot_rows(keys_turned, grad_scores)
            out_ref[start : start + half, first : first + HEAD_DIM] = (
                (grad_turned * SCALE).T.astype(LOW)
            )
            add_keys = dot_rows(grad_scores, queries)
            add_values = dot_rows(attention.astype(LOW), grad_mix)
            grad_keys = add_keys if grad_keys is None else grad_keys + add_keys
            grad_values = add_values if grad_values is None else grad_values + add_values
        key_first = width + first
        value_first = 2 * width + first
        out_ref[:, key_first : key_first + HEAD_DIM] = (grad_keys * SCALE).astype(LOW)
        out_ref[:, value_first : value_first + HEAD_DIM] = grad_values.astype(LOW)


def attention_back(valid_col, qkv, grad_mix):
    return pl.pallas_call(
        attention_back_kernel,
        out_shape=jax.ShapeDtypeStruct(qkv.shape, LOW),
        cost_estimate=attention_cost(qkv.shape[0], grad_mix.shape[1], 5),
        name="attention_back",
    )(valid_col, qkv, grad_mix)


def weight_grad_kernel(layout, *refs):
    out_ref = refs[-1]
    position = 0
    filled = 0
    for chunks, start, cols in layout:
        total = None
        for _ in range(chunks):
            part = dot_first(refs[position][...], refs[position + 1][...])
            total = part if total is None else total + part
            position += 2
        if start > filled:
            out_ref[:, filled:start] = jnp.zeros((out_ref.shape[0], start - filled), LOW)
        out_ref[:, start : start + cols] = total.astype(LOW)
        filled = start + cols


def weight_grads(sections, name):
    width = sections[0][0][0].shape[1]
    block_rows = width // 3
    layout, operands, specs = [], [], []
    start, flops = 0, 0
    for pairs in sections:
        cols = pairs[0][1].shape[1]
        start = -(-start // 128) * 128
        layout.append((len(pairs), start, cols))
        start += cols
        for left_side, right_side in pairs:
            operands += [left_side, right_side]
            flops += 2 * left_side.shape[0] * width * cols
            specs += [
                pl.BlockSpec((left_side.shape[0], block_rows), lambda step: (0, step)),
                pl.BlockSpec(
                    right_side.shape, lambda step: (0, 0), pipeline_mode=pl.Buffered(1)
                ),
            ]
    moved = sum(2 * operand.size for operand in operands) + 2 * width * start
    return pl.pallas_call(
        functools.partial(weight_grad_kernel, tuple(layout)),
        grid=(3,),
        in_specs=specs,
        out_specs=pl.BlockSpec((block_rows, start), lambda step: (step, 0)),
        out_shape=jax.ShapeDtypeStruct((width, start), LOW),
        cost_estimate=pl.CostEstimate(flops=flops, transcendentals=0, bytes_accessed=moved),
        name=name,
    )(*operands)


def sum_everywhere(vector):
    total = vector + swap(vector)
    devices = lax.axis_size("dp")
    step = 1
    while step < devices:
        pairs = [(index, index ^ step) for index in range(devices)]
        total = total + lax.ppermute(total, "dp", pairs)
        step *= 2
    return total


def pad_cols(tensor, width):
    return jnp.pad(tensor, ((0, 0), (0, width - tensor.shape[1])))


def gather_rows(tensor):
    return lax.all_gather(tensor, "dp", axis=0, tiled=True)


def scatter_rows(tensor):
    tensor = with_layout_constraint(tensor, Layout((0, 1)))
    part = lax.psum_scatter(tensor, "dp", scatter_dimension=0, tiled=True)
    return with_layout_constraint(part, Layout((0, 1))).astype(jnp.float32)


def local_pair(
    activations,
    valid_mask,
    first_gain,
    first_shift,
    w_query,
    b_query,
    w_key,
    w_value,
    b_value,
    w_out,
    b_out,
    second_gain,
    second_shift,
    w_up,
    b_up,
    w_down,
    b_down,
    cotangent,
):
    images, half, width = activations.shape
    mp_index = lax.axis_index("mp")
    cols = w_query.shape[1]
    units = w_up.shape[1]
    lane_units = -(-units // 128) * 128
    lane_qkv = -(-3 * cols // 128) * 128
    tokens = images * half
    validity = valid_mask.astype(jnp.float32)
    valid_own = lax.dynamic_slice_in_dim(validity, mp_index * half, half, 1)
    valid_other = lax.dynamic_slice_in_dim(validity, (1 - mp_index) * half, half, 1)
    valid_both = jnp.concatenate([valid_own, valid_other], 1)
    query_bias = lax.dynamic_slice_in_dim(b_query, mp_index * cols, cols)
    value_bias = lax.dynamic_slice_in_dim(b_value, mp_index * cols, cols)
    up_bias = lax.dynamic_slice_in_dim(b_up, mp_index * units, units)
    qkv_bias = jnp.concatenate([query_bias, jnp.zeros_like(query_bias), value_bias])

    qkv_shard = jnp.concatenate([w_query, w_key, w_value], 1).astype(LOW)
    first_full = gather_rows(
        jnp.concatenate([pad_cols(qkv_shard, lane_qkv), w_out.T.astype(LOW)], 1)
    )
    qkv_full = first_full[:, : 3 * cols]
    out_full = first_full[:, lane_qkv:]
    second_full = gather_rows(
        jnp.concatenate(
            [pad_cols(w_up.astype(LOW), lane_units), w_down.T.astype(LOW)], 1
        )
    )
    up_full = second_full[:, :units]
    down_full = second_full[:, lane_units:]

    flat = activations.reshape(tokens, width)
    normed_one, inverse_one = normalize(flat)
    input_own = (normed_one * first_gain + first_shift).astype(LOW)
    input_other = swap(input_own)
    grad_out = (cotangent * valid_own[:, :, None]).reshape(tokens, width)
    grad_b_down = jnp.sum(grad_out, 0)
    grad_rows_own = grad_out.astype(LOW)
    grad_rows_other = swap(grad_rows_own)

    both_one, qkv, mixtures = [], [], []
    residuals, normeds, inverses, lows, crossed = [], [], [], [], []
    for image in range(images):
        own_span = slice(image * half, (image + 1) * half)
        both = jnp.concatenate([input_own[own_span], input_other[own_span]], 0)
        both_one.append(both)
        qkv.append((dot_rows(both, qkv_full) + qkv_bias).astype(LOW))
        mixture = attention_forward(valid_both[image][None, :], qkv[-1])
        if image == 0:
            mixture, grad_rows_other = lax.optimization_barrier((mixture, grad_rows_other))
        mixtures.append(mixture)
        received = swap(dot_last(mixture[half:], out_full).astype(LOW))
        own_part = dot_last(mixture[:half], out_full)
        if image > 0:
            received, own_part, lows[-1] = lax.optimization_barrier(
                (received, own_part, lows[-1])
            )
        residual = activations[image] + (own_part + received.astype(jnp.float32)) + b_out
        normed, inverse = normalize(residual)
        low_rows = (normed * second_gain + second_shift).astype(LOW)
        residuals.append(residual)
        normeds.append(normed)
        inverses.append(inverse)
        lows.append(low_rows)
        crossed.append(swap(low_rows))
    residual = jnp.concatenate(residuals, 0)
    normed_two = jnp.concatenate(normeds, 0)
    inverse_two = jnp.concatenate(inverses, 0)
    rows_own = jnp.concatenate(lows, 0)
    hidden_own = dot_rows(rows_own, up_full) + up_bias
    grad_active_other = dot_rows(grad_rows_other, down_full)
    crossed[-1], hidden_own, grad_active_other = lax.optimization_barrier(
        (crossed[-1], hidden_own, grad_active_other)
    )
    rows_other = jnp.concatenate(crossed, 0)

    hidden_other = dot_rows(rows_other, up_full) + up_bias
    active_other = activate(hidden_other).astype(LOW)
    grad_hidden_other = jax.vjp(activate, hidden_other)[1](grad_active_other)[0].astype(LOW)
    back_other = swap(dot_last(grad_hidden_other, up_full).astype(LOW))
    active_own = activate(hidden_own).astype(LOW)
    grad_active_own = dot_rows(grad_rows_own, down_full)
    grad_hidden_own = jax.vjp(activate, hidden_own)[1](grad_active_own)[0].astype(LOW)
    back_own = dot_last(grad_hidden_own, up_full)
    grad_b_up_here = jnp.sum(grad_hidden_own.astype(jnp.float32), 0) + jnp.sum(
        grad_hidden_other.astype(jnp.float32), 0
    )
    wide_pack = weight_grads(
        (
            ((rows_own, grad_hidden_own), (rows_other, grad_hidden_other)),
            ((grad_rows_own, active_own), (grad_rows_other, active_other)),
        ),
        "wide_grads",
    )
    back_other, wide_pack = lax.optimization_barrier((back_other, wide_pack))
    wide = scatter_rows(wide_pack)

    mlp_other = dot_last(active_other, down_full).astype(LOW)
    mlp_own = dot_last(active_own, down_full)

    grad_input_two = back_own + back_other.astype(jnp.float32)
    grad_second_gain = jnp.sum(grad_input_two * normed_two, 0)
    grad_second_shift = jnp.sum(grad_input_two, 0)
    grad_residual = grad_out + norm_back(grad_input_two, normed_two, inverse_two, second_gain)
    grad_b_out = jnp.sum(grad_residual, 0)
    grad_res_own = grad_residual.astype(LOW)
    spans = [slice(image * half, (image + 1) * half) for image in range(images)]
    grad_res_other = [swap(grad_res_own[span]) for span in spans]
    grad_res_other[0], mlp_other = lax.optimization_barrier((grad_res_other[0], mlp_other))
    mlp_other = swap(mlp_other)
    grad_both, dqkv = [], []
    for image in range(images):
        if image > 0:
            grad_res_other[image], dqkv[-1] = lax.optimization_barrier(
                (grad_res_other[image], dqkv[-1])
            )
        both = jnp.concatenate([grad_res_own[spans[image]], grad_res_other[image]], 0)
        grad_both.append(both)
        grad_mix = dot_rows(both, out_full).astype(LOW)
        dqkv.append(attention_back(valid_both[image][:, None], qkv[image], grad_mix))
    tail_pack = weight_grads(
        (tuple(zip(both_one, dqkv)), tuple(zip(grad_both, mixtures))), "tail_grads"
    )
    dqkv[0], dqkv[1], tail_pack, mlp_other = lax.optimization_barrier(
        (dqkv[0], dqkv[1], tail_pack, mlp_other)
    )
    output = residual + (mlp_own + mlp_other.astype(jnp.float32)) + b_down
    tail_pack, wide = lax.optimization_barrier((tail_pack, wide))
    tail = scatter_rows(tail_pack)
    dqkv_other = jnp.concatenate([grads[half:] for grads in dqkv], 0)
    input_other_part = swap(dot_last(dqkv_other, qkv_full).astype(LOW))
    dqkv_own = jnp.concatenate([grads[:half] for grads in dqkv], 0)
    input_own_part = dot_last(dqkv_own, qkv_full)
    bias_sums = sum(jnp.sum(grads.astype(jnp.float32), 0) for grads in dqkv)
    grad_input_one = input_own_part + input_other_part.astype(jnp.float32)
    grad_first_gain = jnp.sum(grad_input_one * normed_one, 0)
    grad_first_shift = jnp.sum(grad_input_one, 0)
    grad_activations = grad_residual + norm_back(
        grad_input_one, normed_one, inverse_one, first_gain
    )
    vectors = (
        grad_first_gain,
        grad_first_shift,
        widen(bias_sums[:cols], b_query.shape[0], mp_index),
        widen(bias_sums[2 * cols :], b_value.shape[0], mp_index),
        grad_b_out,
        grad_second_gain,
        grad_second_shift,
        widen(grad_b_up_here, b_up.shape[0], mp_index),
        grad_b_down,
    )
    packed = jnp.concatenate(vectors)
    lanes = -(-packed.shape[0] // 1024) * 1024
    packed = jnp.pad(packed, (0, lanes - packed.shape[0])).reshape(-1, 128)
    packed = sum_everywhere(packed).reshape(-1)
    sums, place = [], 0
    for vector in vectors:
        sums.append(packed[place : place + vector.shape[0]])
        place += vector.shape[0]
    return (
        output.reshape(activations.shape),
        grad_activations.reshape(activations.shape),
        sums[0],
        sums[1],
        tail[:, :cols],
        sums[2],
        tail[:, cols : 2 * cols],
        tail[:, 2 * cols : 3 * cols],
        sums[3],
        tail[:, lane_qkv:].T,
        sums[4],
        sums[5],
        sums[6],
        wide[:, :units],
        sums[7],
        wide[:, lane_units:].T,
        sums[8],
    )


def solution(mesh):
    two_way = mesh.shape["mp"] == 2 and mesh.shape["dp"] & (mesh.shape["dp"] - 1) == 0
    step = jax.shard_map(
        local_pair if two_way else local,
        mesh=mesh,
        in_specs=(
            P("dp", "mp", None),
            P("dp", None),
            P(),
            P(),
            P("dp", "mp"),
            P(),
            P("dp", "mp"),
            P("dp", "mp"),
            P(),
            P("mp", "dp"),
            P(),
            P(),
            P(),
            P("dp", "mp"),
            P(),
            P("mp", "dp"),
            P(),
            P("dp", "mp", None),
        ),
        out_specs=(
            P("dp", "mp", None),
            P("dp", "mp", None),
            P(),
            P(),
            P("dp", "mp"),
            P(),
            P("dp", "mp"),
            P("dp", "mp"),
            P(),
            P("mp", "dp"),
            P(),
            P(),
            P(),
            P("dp", "mp"),
            P(),
            P("mp", "dp"),
            P(),
        ),
        check_vma=False,
    )
    return step
```

```python
import functools
import math

import jax
import jax.numpy as jnp
from jax import lax
from jax.experimental import pallas as pl
from jax.experimental.layout import Layout, with_layout_constraint
from jax.sharding import PartitionSpec as P

HEAD_DIM = 72


EPS = 1e-06


def normalize(tensor):
    average = jnp.mean(tensor, -1, keepdims=True)
    centred = tensor - average
    spread = jnp.mean(centred * centred, -1, keepdims=True)
    inverse = lax.rsqrt(spread + EPS)
    return (centred * inverse, inverse)


def norm_back(grad_norm, normed, inverse, norm_gain):
    scaled = grad_norm * norm_gain
    first_mean = jnp.mean(scaled, -1, keepdims=True)
    second_mean = jnp.mean(scaled * normed, -1, keepdims=True)
    return inverse * (scaled - first_mean - normed * second_mean)


def flat_rows(tensor):
    return tensor.reshape(-1, tensor.shape[-1])


def right_dot(left_side, right_side):
    return jnp.dot(flat_rows(left_side), right_side, preferred_element_type=jnp.float32)


def inner_dot(left_side, right_side):
    return lax.dot_general(
        flat_rows(left_side),
        flat_rows(right_side),
        (((0,), (0,)), ((), ())),
        preferred_element_type=jnp.float32,
    )


def transposed_dot(left_side, right_side):
    return lax.dot_general(
        flat_rows(left_side),
        right_side,
        (((1,), (1,)), ((), ())),
        preferred_element_type=jnp.float32,
    )


def activate(hidden):
    return jax.nn.gelu(hidden, approximate=True)


def collect(tensor):
    return lax.all_gather(tensor, "mp", axis=1, tiled=True)


def collect_again(tensor):
    return lax.all_gather(tensor, "mp", axis=1, tiled=True)


def spread_sum(tensor):
    return lax.psum_scatter(
        tensor.astype(jnp.bfloat16), "mp", scatter_dimension=1, tiled=True
    ).astype(jnp.float32)


def widen(vector, length, mp_index):
    return lax.dynamic_update_slice_in_dim(
        jnp.zeros((length,), jnp.float32), vector, mp_index * vector.shape[0], 0
    )


def project(rows, query_full, key_full, value_full, query_bias, value_bias):
    shape = rows.shape[:2] + (query_full.shape[1],)
    queries = (right_dot(rows, query_full) + query_bias).astype(jnp.bfloat16).reshape(shape)
    key_rows = right_dot(rows, key_full).astype(jnp.bfloat16).reshape(shape)
    values = (right_dot(rows, value_full) + value_bias).astype(jnp.bfloat16).reshape(shape)
    return (queries, key_rows, values)


def expand(rows, up_full, up_bias):
    hidden = right_dot(rows, up_full) + up_bias
    return (hidden, activate(hidden).astype(jnp.bfloat16))


def split_heads(tensor):
    return tensor.reshape(tensor.shape[0], tensor.shape[1] // HEAD_DIM, HEAD_DIM)


def scores_of(queries, key_rows):
    raw_scores = jnp.einsum(
        "qhd,khd->hqk",
        split_heads(queries),
        split_heads(key_rows),
        preferred_element_type=jnp.float32,
    )
    return raw_scores * HEAD_DIM ** (-0.5)


def attend_forward(image_block):
    queries, key_rows, values, validity = image_block
    unnorm = validity[None, None, :] * jnp.exp(scores_of(queries, key_rows))
    row_total = jnp.maximum(jnp.sum(unnorm, -1, keepdims=True), 1.0)
    attention = (unnorm / row_total).astype(jnp.bfloat16)
    mixture = jnp.einsum(
        "hqk,khd->qhd", attention, split_heads(values), preferred_element_type=jnp.float32
    )
    return (mixture.reshape(queries.shape).astype(jnp.bfloat16), jnp.log(row_total))


def attend_back(image_block):
    queries, key_rows, values, validity, log_total, grad_mixture = image_block
    attention = validity[None, None, :] * jnp.exp(scores_of(queries, key_rows) - log_total)
    bound = (log_total > 0.0).astype(jnp.float32)
    grad_heads = split_heads(grad_mixture)
    grad_attention = jnp.einsum(
        "qhd,khd->hqk", grad_heads, split_heads(values), preferred_element_type=jnp.float32
    )
    row_delta = bound * jnp.sum(attention * grad_attention, -1, keepdims=True)
    grad_scores = (attention * (grad_attention - row_delta) * HEAD_DIM ** (-0.5)).astype(
        jnp.bfloat16
    )
    grad_queries = jnp.einsum(
        "hqk,khd->qhd", grad_scores, split_heads(key_rows), preferred_element_type=jnp.float32
    )
    grad_keys = jnp.einsum(
        "hqk,qhd->khd", grad_scores, split_heads(queries), preferred_element_type=jnp.float32
    )
    grad_values = jnp.einsum(
        "hqk,qhd->khd",
        attention.astype(jnp.bfloat16),
        grad_heads,
        preferred_element_type=jnp.float32,
    )
    shape = queries.shape
    return (
        grad_queries.reshape(shape).astype(jnp.bfloat16),
        grad_keys.reshape(shape).astype(jnp.bfloat16),
        grad_values.reshape(shape).astype(jnp.bfloat16),
    )


def local(
    activations,
    valid_mask,
    first_gain,
    first_shift,
    w_query,
    b_query,
    w_key,
    w_value,
    b_value,
    w_out,
    b_out,
    second_gain,
    second_shift,
    w_up,
    b_up,
    w_down,
    b_down,
    cotangent,
):
    images, local_rows, width = activations.shape
    mp_index = lax.axis_index("mp")
    head_cols = w_query.shape[1]
    hidden_cols = w_up.shape[1]
    validity = valid_mask.astype(jnp.float32)
    row_valid = lax.dynamic_slice_in_dim(validity, mp_index * local_rows, local_rows, 1)
    query_bias = lax.dynamic_slice_in_dim(b_query, mp_index * head_cols, head_cols)
    value_bias = lax.dynamic_slice_in_dim(b_value, mp_index * head_cols, head_cols)
    up_bias = lax.dynamic_slice_in_dim(b_up, mp_index * hidden_cols, hidden_cols)
    low_type = jnp.bfloat16
    normed_one, inverse_one = normalize(activations)
    input_one = (normed_one * first_gain + first_shift).astype(low_type)
    query_full, key_full, value_full, out_full = (
        lax.all_gather(w_query.astype(low_type), "dp", axis=0, tiled=True),
        lax.all_gather(w_key.astype(low_type), "dp", axis=0, tiled=True),
        lax.all_gather(w_value.astype(low_type), "dp", axis=0, tiled=True),
        lax.all_gather(w_out.astype(low_type), "dp", axis=1, tiled=True),
    )
    rows_one = collect(input_one)
    queries, key_rows, values = project(
        rows_one, query_full, key_full, value_full, query_bias, value_bias
    )
    mixture, log_total = lax.map(attend_forward, (queries, key_rows, values, validity))
    attn_part = right_dot(mixture, out_full).reshape(rows_one.shape)
    residual = activations + spread_sum(attn_part) + b_out
    normed_two, inverse_two = normalize(residual)
    input_two = (normed_two * second_gain + second_shift).astype(low_type)
    up_full, down_full = (
        lax.all_gather(w_up.astype(low_type), "dp", axis=0, tiled=True),
        lax.all_gather(w_down.astype(low_type), "dp", axis=1, tiled=True),
    )
    rows_two = collect(input_two)
    hidden, active = expand(rows_two, up_full, up_bias)
    mlp_part = jnp.dot(active, down_full, preferred_element_type=jnp.float32).reshape(
        rows_two.shape
    )
    output = residual + spread_sum(mlp_part) + b_down
    grad_out = cotangent * row_valid[:, :, None]
    grad_b_down = jnp.sum(grad_out, (0, 1))
    grad_rows_two = collect(grad_out.astype(low_type))
    up_back, down_back = (
        lax.all_gather(w_up.astype(low_type), "dp", axis=0, tiled=True),
        lax.all_gather(w_down.astype(low_type), "dp", axis=1, tiled=True),
    )
    rows_two_back = collect_again(input_two)
    hidden_back, active_back = expand(rows_two_back, up_back, up_bias)
    grad_w_down = inner_dot(active_back, grad_rows_two)
    grad_active = transposed_dot(grad_rows_two, down_back)
    grad_hidden = jax.vjp(activate, hidden_back)[1](grad_active)[0].astype(low_type)
    grad_b_up_here = jnp.sum(grad_hidden.astype(jnp.float32), 0)
    grad_w_up = inner_dot(rows_two_back, grad_hidden)
    grad_input_two = spread_sum(transposed_dot(grad_hidden, up_back).reshape(rows_two.shape))
    grad_second_gain = jnp.sum(grad_input_two * normed_two, (0, 1))
    grad_second_shift = jnp.sum(grad_input_two, (0, 1))
    grad_residual = grad_out + norm_back(grad_input_two, normed_two, inverse_two, second_gain)
    grad_b_out = jnp.sum(grad_residual, (0, 1))
    grad_rows_one = collect(grad_residual.astype(low_type))
    query_back, key_back, value_back, out_back = (
        lax.all_gather(w_query.astype(low_type), "dp", axis=0, tiled=True),
        lax.all_gather(w_key.astype(low_type), "dp", axis=0, tiled=True),
        lax.all_gather(w_value.astype(low_type), "dp", axis=0, tiled=True),
        lax.all_gather(w_out.astype(low_type), "dp", axis=1, tiled=True),
    )
    rows_one_back = collect_again(input_one)
    queries_back, key_rows_back, values_back = project(
        rows_one_back, query_back, key_back, value_back, query_bias, value_bias
    )
    mixture_back, log_total_back = lax.map(
        attend_forward, (queries_back, key_rows_back, values_back, validity)
    )
    grad_w_out = inner_dot(mixture_back, grad_rows_one)
    grad_mixture = (
        transposed_dot(grad_rows_one, out_back).astype(low_type).reshape(queries_back.shape)
    )
    grad_queries, grad_keys, grad_values = lax.map(
        attend_back,
        (queries_back, key_rows_back, values_back, validity, log_total_back, grad_mixture),
    )
    grad_w_query = inner_dot(rows_one_back, grad_queries)
    grad_w_key = inner_dot(rows_one_back, grad_keys)
    grad_w_value = inner_dot(rows_one_back, grad_values)
    grad_b_query_here = jnp.sum(grad_queries.astype(jnp.float32), (0, 1))
    grad_b_value_here = jnp.sum(grad_values.astype(jnp.float32), (0, 1))
    grad_input_part = (
        transposed_dot(grad_queries, query_back)
        + transposed_dot(grad_keys, key_back)
        + transposed_dot(grad_values, value_back)
    )
    grad_input_one = spread_sum(grad_input_part.reshape(rows_one.shape))
    grad_first_gain = jnp.sum(grad_input_one * normed_one, (0, 1))
    grad_first_shift = jnp.sum(grad_input_one, (0, 1))
    grad_activations = grad_residual + norm_back(
        grad_input_one, normed_one, inverse_one, first_gain
    )
    (
        grad_w_query_shard,
        grad_w_key_shard,
        grad_w_value_shard,
        grad_w_out_shard,
        grad_w_up_shard,
        grad_w_down_shard,
    ) = (
        lax.psum_scatter(
            grad_w_query.astype(jnp.bfloat16), "dp", scatter_dimension=0, tiled=True
        ).astype(jnp.float32),
        lax.psum_scatter(
            grad_w_key.astype(jnp.bfloat16), "dp", scatter_dimension=0, tiled=True
        ).astype(jnp.float32),
        lax.psum_scatter(
            grad_w_value.astype(jnp.bfloat16), "dp", scatter_dimension=0, tiled=True
        ).astype(jnp.float32),
        lax.psum_scatter(
            grad_w_out.astype(jnp.bfloat16), "dp", scatter_dimension=1, tiled=True
        ).astype(jnp.float32),
        lax.psum_scatter(
            grad_w_up.astype(jnp.bfloat16), "dp", scatter_dimension=0, tiled=True
        ).astype(jnp.float32),
        lax.psum_scatter(
            grad_w_down.astype(jnp.bfloat16), "dp", scatter_dimension=1, tiled=True
        ).astype(jnp.float32),
    )
    vector_sums = lax.psum(
        (
            grad_first_gain,
            grad_first_shift,
            widen(grad_b_query_here, b_query.shape[0], mp_index),
            widen(grad_b_value_here, b_value.shape[0], mp_index),
            grad_b_out,
            grad_second_gain,
            grad_second_shift,
            widen(grad_b_up_here, b_up.shape[0], mp_index),
            grad_b_down,
        ),
        ("dp", "mp"),
    )
    return (
        output,
        grad_activations,
        vector_sums[0],
        vector_sums[1],
        grad_w_query_shard,
        vector_sums[2],
        grad_w_key_shard,
        grad_w_value_shard,
        vector_sums[3],
        grad_w_out_shard,
        vector_sums[4],
        vector_sums[5],
        vector_sums[6],
        grad_w_up_shard,
        vector_sums[7],
        grad_w_down_shard,
        vector_sums[8],
    )


SCALE = HEAD_DIM ** (-0.5)
SCALE_TWO = SCALE / math.log(2.0)
LOW = jnp.bfloat16


def swap(tensor):
    return lax.ppermute(tensor, "mp", [(0, 1), (1, 0)])


def dot_rows(left_side, right_side):
    return lax.dot_general(
        left_side, right_side, (((1,), (0,)), ((), ())), preferred_element_type=jnp.float32
    )


def dot_last(left_side, right_side):
    return lax.dot_general(
        left_side, right_side, (((1,), (1,)), ((), ())), preferred_element_type=jnp.float32
    )


def dot_first(left_side, right_side):
    return lax.dot_general(
        left_side, right_side, (((0,), (0,)), ((), ())), preferred_element_type=jnp.float32
    )


def head_columns(ref, part, head, width):
    first = part * width + head * HEAD_DIM
    return ref[:, first : first + HEAD_DIM]


def attention_cost(rows, width, dots):
    heads = width // HEAD_DIM
    return pl.CostEstimate(
        flops=dots * heads * 2 * rows * rows * 256,
        transcendentals=heads * rows * rows,
        bytes_accessed=10 * rows * width,
    )


def attention_kernel(valid_ref, qkv_ref, mix_ref):
    rows, width = mix_ref.shape
    half = rows // 2
    valid = valid_ref[...]
    for head in range(width // HEAD_DIM):
        first = head * HEAD_DIM
        keys = head_columns(qkv_ref, 1, head, width)
        values = head_columns(qkv_ref, 2, head, width)
        for start in (0, half):
            queries = qkv_ref[start : start + half, first : first + HEAD_DIM]
            unnorm = jnp.exp2(dot_last(queries, keys) * SCALE_TWO) * valid
            row_total = jnp.maximum(jnp.sum(unnorm, -1, keepdims=True), 1.0)
            attention = (unnorm * (1.0 / row_total)).astype(LOW)
            mix_ref[start : start + half, first : first + HEAD_DIM] = dot_rows(
                attention, values
            ).astype(LOW)


def attention_forward(valid_row, qkv):
    rows, width = qkv.shape[0], qkv.shape[1] // 3
    return pl.pallas_call(
        attention_kernel,
        out_shape=jax.ShapeDtypeStruct((rows, width), LOW),
        cost_estimate=attention_cost(rows, width, 2),
        name="attention_forward",
    )(valid_row, qkv)


def attention_back_kernel(valid_ref, qkv_ref, grad_ref, out_ref):
    rows, width = grad_ref.shape
    half = rows // 2
    valid = valid_ref[...]
    for head in range(width // HEAD_DIM):
        first = head * HEAD_DIM
        keys = head_columns(qkv_ref, 1, head, width)
        values = head_columns(qkv_ref, 2, head, width)
        keys_turned = keys.T
        grad_keys = None
        grad_values = None
        for start in (0, half):
            queries = qkv_ref[start : start + half, first : first + HEAD_DIM]
            grad_mix = grad_ref[start : start + half, first : first + HEAD_DIM]
            unnorm = jnp.exp2(dot_last(keys, queries) * SCALE_TWO) * valid
            row_total = jnp.maximum(jnp.sum(unnorm, 0, keepdims=True), 1.0)
            attention = unnorm * (1.0 / row_total)
            bound = jnp.where(row_total > 1.0, 1.0, 0.0)
            grad_attention = dot_last(values, grad_mix)
            row_delta = bound * jnp.sum(attention * grad_attention, 0, keepdims=True)
            grad_scores = (attention * (grad_attention - row_delta)).astype(LOW)
            grad_turned = dot_rows(keys_turned, grad_scores)
            out_ref[start : start + half, first : first + HEAD_DIM] = (
                (grad_turned * SCALE).T.astype(LOW)
            )
            add_keys = dot_rows(grad_scores, queries)
            add_values = dot_rows(attention.astype(LOW), grad_mix)
            grad_keys = add_keys if grad_keys is None else grad_keys + add_keys
            grad_values = add_values if grad_values is None else grad_values + add_values
        key_first = width + first
        value_first = 2 * width + first
        out_ref[:, key_first : key_first + HEAD_DIM] = (grad_keys * SCALE).astype(LOW)
        out_ref[:, value_first : value_first + HEAD_DIM] = grad_values.astype(LOW)


def attention_back(valid_col, qkv, grad_mix):
    return pl.pallas_call(
        attention_back_kernel,
        out_shape=jax.ShapeDtypeStruct(qkv.shape, LOW),
        cost_estimate=attention_cost(qkv.shape[0], grad_mix.shape[1], 5),
        name="attention_back",
    )(valid_col, qkv, grad_mix)


def chip_ring(devices):
    deep = devices // 4
    return [2 * place for place in range(deep)] + [
        2 * (deep - 1 - place) + 1 for place in range(deep)
    ]


def ring_scatter(tensor, between):
    devices = lax.axis_size("dp")
    order = chip_ring(devices)
    chips = len(order)
    place = [order.index(chip) for chip in range(chips)]
    index = lax.axis_index("dp")
    core = index % 2
    position = jnp.array(place, jnp.int32)[index // 2]
    rows = tensor.shape[0] // devices
    order_array = jnp.array(order + order, jnp.int32)

    def chunk(ahead, which):
        start = (order_array[position + ahead] * 2 + which) * rows
        return lax.dynamic_slice_in_dim(tensor, start, rows, 0)

    def moves(step):
        return [
            (2 * order[place] + one, 2 * order[(place + step) % chips] + one)
            for place in range(chips)
            for one in range(2)
        ]

    twins = [(one, one ^ 1) for one in range(devices)]
    up, down = chips // 2, chips - chips // 2 - 1
    ahead_up = list(range(up, 0, -1))
    ahead_down = list(range(chips - down, chips))
    groups, rest = [], []
    for turn in range(max(up, down)):
        group = [ahead_up[turn]] if turn < up else []
        group += [ahead_down[turn]] if turn < down else []
        groups.append(group)
    groups[-1].append(0)
    sums = {}
    for group in groups:
        twin_rows = jnp.concatenate([chunk(one, 1 - core) for one in group], 0)
        sent = lax.ppermute(twin_rows, "dp", twins)
        for slot, one in enumerate(group):
            part = sent[slot * rows : (slot + 1) * rows].astype(jnp.float32)
            sums[one] = chunk(one, core).astype(jnp.float32) + part
    forward = backward = None
    for turn in range(max(up, down)):
        value = sums[ahead_up[turn]]
        value = value if forward is None else value + forward.astype(jnp.float32)
        (value,) = between(turn, (value,))
        forward = lax.ppermute(value.astype(LOW), "dp", moves(1))
        if turn < down:
            value = sums[ahead_down[turn]]
            value = value if backward is None else value + backward.astype(jnp.float32)
            backward = lax.ppermute(value.astype(LOW), "dp", moves(-1))
    total = sums[0] + forward.astype(jnp.float32) + backward.astype(jnp.float32)
    return between(max(up, down), (total,))[0]


def weight_grad_kernel(layout, *refs):
    out_ref = refs[-1]
    position = 0
    filled = 0
    for chunks, start, cols in layout:
        total = None
        for _ in range(chunks):
            part = dot_first(refs[position][...], refs[position + 1][...])
            total = part if total is None else total + part
            position += 2
        if start > filled:
            out_ref[:, filled:start] = jnp.zeros((out_ref.shape[0], start - filled), LOW)
        out_ref[:, start : start + cols] = total.astype(LOW)
        filled = start + cols


def weight_grads(sections, name):
    width = sections[0][0][0].shape[1]
    block_rows = width // 3
    layout, operands, specs = [], [], []
    start, flops = 0, 0
    for pairs in sections:
        cols = pairs[0][1].shape[1]
        start = -(-start // 128) * 128
        layout.append((len(pairs), start, cols))
        start += cols
        for left_side, right_side in pairs:
            operands += [left_side, right_side]
            flops += 2 * left_side.shape[0] * width * cols
            specs += [
                pl.BlockSpec((left_side.shape[0], block_rows), lambda step: (0, step)),
                pl.BlockSpec(
                    right_side.shape, lambda step: (0, 0), pipeline_mode=pl.Buffered(1)
                ),
            ]
    moved = sum(2 * operand.size for operand in operands) + 2 * width * start
    return pl.pallas_call(
        functools.partial(weight_grad_kernel, tuple(layout)),
        grid=(3,),
        in_specs=specs,
        out_specs=pl.BlockSpec((block_rows, start), lambda step: (step, 0)),
        out_shape=jax.ShapeDtypeStruct((width, start), LOW),
        cost_estimate=pl.CostEstimate(flops=flops, transcendentals=0, bytes_accessed=moved),
        name=name,
    )(*operands)


def sum_round(vector, bits):
    devices = lax.axis_size("dp") * lax.axis_size("mp")

    def other(mask):
        pairs = [(index, index ^ mask) for index in range(devices)]
        return lax.ppermute(vector, ("dp", "mp"), pairs)

    if len(bits) == 1:
        return vector + other(bits[0])
    near = vector + other(bits[0])
    far = other(bits[1]) + other(bits[0] | bits[1])
    return near + far


def sum_rounds(devices):
    bits = [1 << place for place in range(devices.bit_length() - 1)]
    return [bits[place : place + 2] for place in range(0, len(bits), 2)]


def pad_cols(tensor, width):
    return jnp.pad(tensor, ((0, 0), (0, width - tensor.shape[1])))


def gather_rows(tensor):
    return lax.all_gather(tensor, "dp", axis=0, tiled=True)


def scatter_rows(tensor):
    tensor = with_layout_constraint(tensor, Layout((0, 1)))
    part = lax.psum_scatter(tensor, "dp", scatter_dimension=0, tiled=True)
    return with_layout_constraint(part, Layout((0, 1))).astype(jnp.float32)


def local_pair(
    activations,
    valid_mask,
    first_gain,
    first_shift,
    w_query,
    b_query,
    w_key,
    w_value,
    b_value,
    w_out,
    b_out,
    second_gain,
    second_shift,
    w_up,
    b_up,
    w_down,
    b_down,
    cotangent,
):
    images, half, width = activations.shape
    mp_index = lax.axis_index("mp")
    cols = w_query.shape[1]
    units = w_up.shape[1]
    lane_units = -(-units // 128) * 128
    lane_qkv = -(-3 * cols // 128) * 128
    tokens = images * half
    validity = valid_mask.astype(jnp.float32)
    valid_own = lax.dynamic_slice_in_dim(validity, mp_index * half, half, 1)
    valid_other = lax.dynamic_slice_in_dim(validity, (1 - mp_index) * half, half, 1)
    valid_both = jnp.concatenate([valid_own, valid_other], 1)
    query_bias = lax.dynamic_slice_in_dim(b_query, mp_index * cols, cols)
    value_bias = lax.dynamic_slice_in_dim(b_value, mp_index * cols, cols)
    up_bias = lax.dynamic_slice_in_dim(b_up, mp_index * units, units)
    qkv_bias = jnp.concatenate([query_bias, jnp.zeros_like(query_bias), value_bias])

    qkv_shard = jnp.concatenate([w_query, w_key, w_value], 1).astype(LOW)
    first_full = gather_rows(
        jnp.concatenate([pad_cols(qkv_shard, lane_qkv), w_out.T.astype(LOW)], 1)
    )
    qkv_full = first_full[:, : 3 * cols]
    out_full = first_full[:, lane_qkv:]
    second_full = gather_rows(
        jnp.concatenate(
            [pad_cols(w_up.astype(LOW), lane_units), w_down.T.astype(LOW)], 1
        )
    )
    up_full = second_full[:, :units]
    down_full = second_full[:, lane_units:]

    flat = activations.reshape(tokens, width)
    normed_one, inverse_one = normalize(flat)
    input_own = (normed_one * first_gain + first_shift).astype(LOW)
    input_other = swap(input_own)
    grad_out = (cotangent * valid_own[:, :, None]).reshape(tokens, width)
    grad_b_down = jnp.sum(grad_out, 0)
    grad_rows_own = grad_out.astype(LOW)
    grad_rows_other = swap(grad_rows_own)

    both_one, qkv, mixtures = [], [], []
    residuals, normeds, inverses, lows, crossed = [], [], [], [], []
    for image in range(images):
        own_span = slice(image * half, (image + 1) * half)
        both = jnp.concatenate([input_own[own_span], input_other[own_span]], 0)
        both_one.append(both)
        qkv.append((dot_rows(both, qkv_full) + qkv_bias).astype(LOW))
        mixture = attention_forward(valid_both[image][None, :], qkv[-1])
        if image == 0:
            mixture, grad_rows_other = lax.optimization_barrier((mixture, grad_rows_other))
        mixtures.append(mixture)
        received = swap(dot_last(mixture[half:], out_full).astype(LOW))
        own_part = dot_last(mixture[:half], out_full)
        if image > 0:
            received, own_part, lows[-1] = lax.optimization_barrier(
                (received, own_part, lows[-1])
            )
        residual = activations[image] + (own_part + received.astype(jnp.float32)) + b_out
        normed, inverse = normalize(residual)
        low_rows = (normed * second_gain + second_shift).astype(LOW)
        residuals.append(residual)
        normeds.append(normed)
        inverses.append(inverse)
        lows.append(low_rows)
        crossed.append(swap(low_rows))
    residual = jnp.concatenate(residuals, 0)
    normed_two = jnp.concatenate(normeds, 0)
    inverse_two = jnp.concatenate(inverses, 0)
    rows_own = jnp.concatenate(lows, 0)
    hidden_own = dot_rows(rows_own, up_full) + up_bias
    grad_active_other = dot_rows(grad_rows_other, down_full)
    crossed[-1], hidden_own, grad_active_other = lax.optimization_barrier(
        (crossed[-1], hidden_own, grad_active_other)
    )
    rows_other = jnp.concatenate(crossed, 0)

    hidden_other = dot_rows(rows_other, up_full) + up_bias
    active_other = activate(hidden_other).astype(LOW)
    grad_hidden_other = jax.vjp(activate, hidden_other)[1](grad_active_other)[0].astype(LOW)
    back_other = swap(dot_last(grad_hidden_other, up_full).astype(LOW))
    active_own = activate(hidden_own).astype(LOW)
    grad_active_own = dot_rows(grad_rows_own, down_full)
    grad_hidden_own = jax.vjp(activate, hidden_own)[1](grad_active_own)[0].astype(LOW)
    back_own = dot_last(grad_hidden_own, up_full)
    grad_b_up_here = jnp.sum(grad_hidden_own.astype(jnp.float32), 0) + jnp.sum(
        grad_hidden_other.astype(jnp.float32), 0
    )
    wide_pack = weight_grads(
        (
            ((rows_own, grad_hidden_own), (rows_other, grad_hidden_other)),
            ((grad_rows_own, active_own), (grad_rows_other, active_other)),
        ),
        "wide_grads",
    )
    back_other, wide_pack = lax.optimization_barrier((back_other, wide_pack))
    wide = scatter_rows(wide_pack)

    spans = [slice(image * half, (image + 1) * half) for image in range(images)]
    mlp_other = dot_last(active_other, down_full).astype(LOW)

    grad_input_two = back_own + back_other.astype(jnp.float32)
    grad_second_gain = jnp.sum(grad_input_two * normed_two, 0)
    grad_second_shift = jnp.sum(grad_input_two, 0)
    grad_residual = grad_out + norm_back(grad_input_two, normed_two, inverse_two, second_gain)
    grad_b_out = jnp.sum(grad_residual, 0)
    grad_res_own = grad_residual.astype(LOW)
    grad_res_other = [swap(grad_res_own[span]) for span in spans]
    grad_res_other[0], mlp_other = lax.optimization_barrier((grad_res_other[0], mlp_other))
    mlp_received = [swap(mlp_other[span]) for span in spans]
    grad_both, dqkv, received = [], [], []
    for image in range(images):
        both = jnp.concatenate([grad_res_own[spans[image]], grad_res_other[image]], 0)
        grad_both.append(both)
        grad_mix = dot_rows(both, out_full).astype(LOW)
        grads = attention_back(valid_both[image][:, None], qkv[image], grad_mix)
        grads, mlp_received[image] = lax.optimization_barrier((grads, mlp_received[image]))
        part = dot_last(grads[half:], qkv_full).astype(LOW)
        received.append(swap(part))
        if image + 1 < images:
            grad_res_other[image + 1], grads, part = lax.optimization_barrier(
                (grad_res_other[image + 1], grads, part)
            )
        else:
            grads, part, received[0] = lax.optimization_barrier((grads, part, received[0]))
        dqkv.append(grads)
    tail_pack = weight_grads(
        (tuple(zip(both_one, dqkv)), tuple(zip(grad_both, mixtures))), "tail_grads"
    )
    rounds = sum_rounds(lax.axis_size("dp") * lax.axis_size("mp"))
    held = {"wide": wide, "received": received[-1]}
    held |= {f"active_{image}": active_own[spans[image]] for image in range(images)}

    def finish(image):
        mlp_part = dot_last(held.pop(f"active_{image}"), down_full)
        mlp_part = mlp_part + mlp_received[image].astype(jnp.float32)
        held[f"output_{image}"] = residuals[image] + mlp_part + b_down

    def finish_input():
        input_own_part = [dot_last(grads[:half], qkv_full) for grads in dqkv]
        bias_sums = sum(jnp.sum(grads.astype(jnp.float32), 0) for grads in dqkv)
        grad_input_one = jnp.concatenate(
            [own + other.astype(jnp.float32) for own, other in zip(input_own_part, [*received[:-1], held["received"]])], 0
        )
        vectors = (
            jnp.sum(grad_input_one * normed_one, 0),
            jnp.sum(grad_input_one, 0),
            widen(bias_sums[:cols], b_query.shape[0], mp_index),
            widen(bias_sums[2 * cols :], b_value.shape[0], mp_index),
            grad_b_out,
            grad_second_gain,
            grad_second_shift,
            widen(grad_b_up_here, b_up.shape[0], mp_index),
            grad_b_down,
        )
        packed = jnp.concatenate(vectors)
        lanes = -(-packed.shape[0] // 1024) * 1024
        packed = jnp.pad(packed, (0, lanes - packed.shape[0])).reshape(-1, 128)
        held["packed"], held["vectors"], held["input"] = packed, vectors, grad_input_one

    def tie(values, *names):
        tied = lax.optimization_barrier((*values, *(held[name] for name in names)))
        held.update(zip(names, tied[len(values) :]))
        return tied[: len(values)]

    def between(turn, values):
        if turn == 0:
            values = tie(values, "received")
            finish_input()
            return values
        values = tie(values, "packed")
        if turn <= len(rounds):
            held["packed"] = sum_round(held["packed"], rounds[turn - 1])
        if turn == 2:
            values = tie(values, "active_0")
            finish(0)
        if turn == 3:
            values = tie(values, "output_0", *(f"active_{one}" for one in range(1, images)))
            for image in range(1, images):
                finish(image)
        if turn == 4:
            values = tie(values, "wide", *(f"output_{one}" for one in range(1, images)))
        return values

    tail = ring_scatter(tail_pack, between)
    wide, packed, vectors = held["wide"], held["packed"], held["vectors"]
    grad_input_one = held["input"]
    output = jnp.stack([held[f"output_{image}"] for image in range(images)])
    grad_activations = grad_residual + norm_back(
        grad_input_one, normed_one, inverse_one, first_gain
    )
    packed = packed.reshape(-1)
    sums, place = [], 0
    for vector in vectors:
        sums.append(packed[place : place + vector.shape[0]])
        place += vector.shape[0]
    return (
        output,
        grad_activations.reshape(activations.shape),
        sums[0],
        sums[1],
        tail[:, :cols],
        sums[2],
        tail[:, cols : 2 * cols],
        tail[:, 2 * cols : 3 * cols],
        sums[3],
        tail[:, lane_qkv:].T,
        sums[4],
        sums[5],
        sums[6],
        wide[:, :units],
        sums[7],
        wide[:, lane_units:].T,
        sums[8],
    )


def solution(mesh):
    two_way = mesh.shape["mp"] == 2 and mesh.shape["dp"] == 16
    step = jax.shard_map(
        local_pair if two_way else local,
        mesh=mesh,
        in_specs=(
            P("dp", "mp", None),
            P("dp", None),
            P(),
            P(),
            P("dp", "mp"),
            P(),
            P("dp", "mp"),
            P("dp", "mp"),
            P(),
            P("mp", "dp"),
            P(),
            P(),
            P(),
            P("dp", "mp"),
            P(),
            P("mp", "dp"),
            P(),
            P("dp", "mp", None),
        ),
        out_specs=(
            P("dp", "mp", None),
            P("dp", "mp", None),
            P(),
            P(),
            P("dp", "mp"),
            P(),
            P("dp", "mp"),
            P("dp", "mp"),
            P(),
            P("mp", "dp"),
            P(),
            P(),
            P(),
            P("dp", "mp"),
            P(),
            P("mp", "dp"),
            P(),
        ),
        check_vma=False,
    )
    return step
```
